32 devices in a mesh: dp: 8 (over y, x, core), exch: 4 (over z).
Axes of the slice: x: 2, y: 2, z: 4, core: 2. Of those that a mesh axis runs over, the one named last changes fastest.
Arguments:
- x_raw: bfloat16 [1024, 2048], P('exch', 'dp'), may hold values from -6 to 6
- bc_raw: bfloat16 [1024, 256], P(('exch', 'dp')), may hold values from -6 to 6
- dt_raw: bfloat16 [32, 1024], P('dp', 'exch'), may hold values from -4 to 4
- cotangent: bfloat16 [1024, 2048], P('exch', 'dp'), may hold values from -6 to 6
- ssm_state: bfloat16 [8, 32, 64, 128], P('exch', 'dp'), may hold values from -0.625 to 0.625
- conv_x_state: bfloat16 [8, 3, 2048], P('exch', None, 'dp'), may hold values from -6 to 6
- conv_bc_state: bfloat16 [8, 3, 256], P('exch'), may hold values from -6 to 6
- owner: int32 [8], P('exch'), may hold values from 0 to 3, as said below
- resp_len: int32 [8], P('exch'), may hold values from 32 to 128, as said below
- conv_x_weight: float32 [4, 2048], P(None, 'dp'), may hold values from -3 to 3
- conv_bc_weight: float32 [4, 256], replicated, may hold values from -3 to 3
- dt_bias: float32 [32], P('dp'), may hold values from -5 to -3
- a_log: float32 [32], P('dp'), may hold values from -2.3 to 2.1
- skip_d: float32 [32], P('dp'), may hold values from 0.5 to 1.5
Outputs:
- grad_x: bfloat16 [1024, 2048], P('exch', 'dp')
- grad_bc: bfloat16 [1024, 256], P(('exch', 'dp'))
- grad_dt: bfloat16 [32, 1024], P('dp', 'exch')
- grad_conv_x: float32 [4, 2048], P(None, 'dp')
- grad_conv_bc: float32 [4, 256], replicated
- grad_heads: float32 [3, 32], P(None, 'dp')
The draws below stay inside these ranges and needn't reach their ends.
Inputs may be any that keep to these rules, and one draw needn't show every extreme that they name: `owner`: among the 2 prompts of one holder (an aligned block along exch) no learner index occurs more than 1 times, and some learner index occurs exactly 1 times; over all 8 prompts every learner index occurs exactly 2 times. `resp_len`: every learner's block of 2 responses holds a response of length 128.
All inputs are finite; a program needn't handle non-finite values.
Results may differ from the reference program's by a relative error of at most 0.001.
Values may be sent and summed in bfloat16 or wider, within the bound.
A program may use at most 64 MiB of HBM per device.

```python
import jax
import jax.numpy as jnp
from jax import lax

HDIM = 64
NSTATE = 128
KCONV = 4
HEADS_GROUP = 32
SPAN = 128
GROUP = 1
CAP = 1
L = 128
P_DEV = 2
PROMPTS = 8
RESP_DEV = 2
RESPONSES = 8
TOK_DEV = 256
TOKENS = 1024
HEADS = 32
NGROUPS = 1
N_EXCH = 4


def draw_owner(key, part):
    holders = PROMPTS // P_DEV
    order = jax.random.permutation(jax.random.fold_in(key, 11), holders)
    entry = jnp.arange(P_DEV)
    which = jnp.where(entry < CAP, 0, entry - CAP + 1)
    shifts = order[which]
    base = jax.random.fold_in(key, 12)
    holder_keys = jax.vmap(lambda holder: jax.random.fold_in(base, holder))(jnp.arange(holders))
    shuffles = jax.vmap(lambda sub: jax.random.permutation(sub, P_DEV))(holder_keys)
    owners = (jnp.arange(holders)[:, None] + shifts[shuffles]) % holders
    return owners.reshape(-1).astype(jnp.int32)


def draw_resp_len(key, part):
    lengths = jax.random.randint(jax.random.fold_in(key, 21), (RESPONSES,), L // 4, L + 1)
    blocks = RESPONSES // RESP_DEV
    chosen = jax.random.randint(jax.random.fold_in(key, 22), (blocks,), 0, RESP_DEV)
    longest = (jnp.arange(RESP_DEV)[None, :] == chosen[:, None]).reshape(-1)
    return jnp.where(longest, L, lengths).astype(jnp.int32)


def block_levels(stream_key, extent, split, low, largest):
    loudness = 1.0
    for position, shards_of in split:
        steps = jax.random.uniform(jax.random.fold_in(jax.random.fold_in(stream_key, 6), position), (shards_of,), jnp.float32, low / len(split), largest / len(split))
        loudness = loudness * jnp.repeat(jnp.exp(steps), extent[position] // shards_of).reshape((-1,) + (1,) * (len(extent) - 1 - position))
    return loudness


def centred(rng, dims, scale, most, shards=(), kind=jnp.bfloat16):
    entries = jax.random.normal(rng, dims, jnp.float32) * scale
    if len(shards) > 0:
        entries = block_levels(rng, dims, shards, -0.22, 0.18) * entries
    return jnp.clip(entries, min=-most, max=most).astype(kind)


def setup_inputs(seed: int = 0) -> dict:
    seeds = jax.random.split(jax.random.key(seed), 15)
    x_raw = centred(seeds[0], (TOKENS, HEADS * HDIM), 1.0, 6.0, ((0, 4), (1, 8)))
    bc_raw = centred(seeds[1], (TOKENS, NGROUPS * 2 * NSTATE), 1.0, 6.0, ((0, 32),))
    dt_raw = centred(seeds[2], (HEADS, TOKENS), 1.0, 4.0, ((0, 8), (1, 4)))
    cotangent = centred(seeds[3], (TOKENS, HEADS * HDIM), 1.0, 6.0, ((0, 4), (1, 8)))
    ssm_state = centred(seeds[4], (PROMPTS, HEADS, HDIM, NSTATE), 0.1, 0.625, ((0, 4), (1, 8)))
    conv_x_state = centred(seeds[5], (PROMPTS, KCONV - 1, HEADS * HDIM), 1.0, 6.0, ((0, 4), (2, 8)))
    conv_bc_state = centred(seeds[6], (PROMPTS, KCONV - 1, NGROUPS * 2 * NSTATE), 1.0, 6.0, ((0, 4),))
    owner = draw_owner(jax.random.fold_in(seeds[14], 71), 0)
    resp_len = draw_resp_len(jax.random.fold_in(seeds[14], 71), 0)
    conv_x_weight = centred(seeds[9], (KCONV, HEADS * HDIM), KCONV ** -0.5, 3.0, ((1, 8),), jnp.float32)
    conv_bc_weight = centred(seeds[10], (KCONV, NGROUPS * 2 * NSTATE), KCONV ** -0.5, 3.0, (), jnp.float32)
    dt_bias = jnp.clip(-5.0 + 2.0 * jax.random.uniform(seeds[11], (HEADS,), jnp.float32) ** block_levels(seeds[11], (HEADS,), ((0, 8),), -0.2, 0.2), -5.0, -3.0)
    a_log = jnp.clip(-2.3 + 4.3999998569488525 * jax.random.uniform(seeds[12], (HEADS,), jnp.float32) ** block_levels(seeds[12], (HEADS,), ((0, 8),), -0.2, 0.2), -2.3, 2.1)
    skip_d = jnp.clip(0.5 + 1.0 * jax.random.uniform(seeds[13], (HEADS,), jnp.float32) ** block_levels(seeds[13], (HEADS,), ((0, 8),), -0.2, 0.2), 0.5, 1.5)
    return {"x_raw": x_raw, "bc_raw": bc_raw, "dt_raw": dt_raw, "cotangent": cotangent, "ssm_state": ssm_state, "conv_x_state": conv_x_state, "conv_bc_state": conv_bc_state, "owner": owner, "resp_len": resp_len, "conv_x_weight": conv_x_weight, "conv_bc_weight": conv_bc_weight, "dt_bias": dt_bias, "a_log": a_log, "skip_d": skip_d}


PRECISE = lax.Precision.HIGHEST

def conv_pre(raw, state, weight):
    padded = jnp.concatenate([state, raw], axis=1)
    length = raw.shape[1]
    total = padded[:, 0:length] * weight[0]
    for offset in range(1, weight.shape[0]):
        total = total + padded[:, offset:offset + length] * weight[offset]
    return total

def ssd_output(values, proj_b, proj_c, steps, rate, skip, start, block):
    rows, length, heads, width = values.shape
    count = length // block
    value_blocks = values.reshape(rows, count, block, heads, width)
    b_blocks = proj_b.reshape(rows, count, block, proj_b.shape[-1])
    c_blocks = proj_c.reshape(rows, count, block, proj_c.shape[-1])
    step_blocks = steps.reshape(rows, count, block, heads)
    logs = jnp.cumsum(-rate * step_blocks, axis=2)
    causal = jnp.tril(jnp.ones((block, block), jnp.float32))
    spread = logs[:, :, :, None, :] - logs[:, :, None, :, :]
    decays = jnp.exp(jnp.where(causal[:, :, None] > 0.5, spread, 0.0)) * causal[:, :, None]
    scores = jnp.einsum('rntk,rnsk->rnts', c_blocks, b_blocks, precision=PRECISE)
    weighted = value_blocks * step_blocks[..., None]
    mixing = scores[..., None] * decays
    intra = jnp.einsum('rntsh,rnshp->rnthp', mixing, weighted, precision=PRECISE)
    tails = jnp.exp(logs[:, :, -1:, :] - logs)
    gains = jnp.einsum('rnshp,rnsk->rnhpk', weighted * tails[..., None], b_blocks, precision=PRECISE)
    state = start
    pieces = []
    for index in range(count):
        entry = jnp.exp(logs[:, index])
        carried = jnp.einsum('rtk,rhpk->rthp', c_blocks[:, index], state, precision=PRECISE)
        pieces.append(carried * entry[..., None])
        if index + 1 < count:
            state = state * jnp.exp(logs[:, index, -1])[:, :, None, None] + gains[:, index]
    inter = jnp.stack(pieces, axis=1)
    output = intra + inter + skip[:, None] * value_blocks
    return output.reshape(rows, length, heads, width)

def window_loss(x_rows, bc_act, dt_rows, x_weight, bias, decay_log, skip, x_prev, start, cotan, mask, heads, block):
    x_act = jax.nn.silu(conv_pre(x_rows, x_prev, x_weight))
    rows, length, channels = x_rows.shape
    values = x_act.reshape(rows, length, heads, channels // heads)
    half = bc_act.shape[-1] // 2
    steps = jax.nn.softplus(dt_rows + bias)
    output = ssd_output(values, bc_act[..., :half], bc_act[..., half:], steps, jnp.exp(decay_log), skip, start, block)
    return jnp.sum(output.reshape(rows, length, channels) * cotan * mask[..., None])

def reference(x_raw, bc_raw, dt_raw, cotangent, ssm_state, conv_x_state, conv_bc_state, owner, resp_len, conv_x_weight, conv_bc_weight, dt_bias, a_log, skip_d):
    order = jnp.argsort(owner, stable=True).astype(jnp.int32).reshape(N_EXCH, P_DEV)
    group_width = HEADS_GROUP * HDIM
    pair_width = 2 * NSTATE

    def per_slice(flat):
        learner = flat // NGROUPS
        my_group = flat % NGROUPS
        take = jnp.repeat(order[learner], GROUP)
        first = learner * TOK_DEV
        head_first = my_group * HEADS_GROUP
        col_first = my_group * group_width
        bc_first = my_group * pair_width
        x_rows = lax.dynamic_slice(x_raw, (first, col_first), (TOK_DEV, group_width)).astype(jnp.float32).reshape(RESP_DEV, L, group_width)
        bc_rows = lax.dynamic_slice(bc_raw, (first, bc_first), (TOK_DEV, pair_width)).astype(jnp.float32).reshape(RESP_DEV, L, pair_width)
        cot_rows = lax.dynamic_slice(cotangent, (first, col_first), (TOK_DEV, group_width)).astype(jnp.float32).reshape(RESP_DEV, L, group_width)
        dt_rows = lax.dynamic_slice(dt_raw, (head_first, first), (HEADS_GROUP, TOK_DEV)).astype(jnp.float32).T.reshape(RESP_DEV, L, HEADS_GROUP)
        lengths = lax.dynamic_slice_in_dim(resp_len, learner * RESP_DEV, RESP_DEV, 0)
        live_mask = (jnp.arange(L, dtype=jnp.int32)[None, :] < lengths[:, None]).astype(jnp.float32)
        start_state = lax.dynamic_slice_in_dim(ssm_state, head_first, HEADS_GROUP, 1)[take].astype(jnp.float32)
        x_prev = lax.dynamic_slice_in_dim(conv_x_state, col_first, group_width, 2)[take].astype(jnp.float32)
        bc_prev = lax.dynamic_slice_in_dim(conv_bc_state, bc_first, pair_width, 2)[take].astype(jnp.float32)
        x_weight = lax.dynamic_slice_in_dim(conv_x_weight, col_first, group_width, 1)
        bc_weight = lax.dynamic_slice_in_dim(conv_bc_weight, bc_first, pair_width, 1)
        bias_part = lax.dynamic_slice_in_dim(dt_bias, head_first, HEADS_GROUP, 0)
        decay_part = lax.dynamic_slice_in_dim(a_log, head_first, HEADS_GROUP, 0)
        skip_part = lax.dynamic_slice_in_dim(skip_d, head_first, HEADS_GROUP, 0)

        def total(x_in, bc_in, dt_in, xw_in, bcw_in, bias, decay_log, skip):
            bc_act = jax.nn.silu(conv_pre(bc_in, bc_prev, bcw_in))
            return window_loss(x_in, bc_act, dt_in, xw_in, bias, decay_log, skip, x_prev, start_state, cot_rows, live_mask, HEADS_GROUP, SPAN)
        return jax.grad(total, argnums=(0, 1, 2, 3, 4, 5, 6, 7))(x_rows, bc_rows, dt_rows, x_weight, bc_weight, bias_part, decay_part, skip_part)
    grad_xr, grad_bcr, grad_dtr, grad_wx, grad_wbc, grad_bias, grad_decay, grad_skip = lax.map(per_slice, jnp.arange(N_EXCH * NGROUPS, dtype=jnp.int32))
    grad_x = grad_xr.reshape(N_EXCH, NGROUPS, TOK_DEV, group_width).transpose(0, 2, 1, 3).reshape(TOKENS, HEADS * HDIM).astype(jnp.bfloat16)
    grad_bc = grad_bcr.reshape(N_EXCH, NGROUPS, TOK_DEV, pair_width).transpose(0, 2, 1, 3).reshape(TOKENS, NGROUPS * pair_width).astype(jnp.bfloat16)
    grad_dt = grad_dtr.reshape(N_EXCH, NGROUPS, TOK_DEV, HEADS_GROUP).transpose(1, 3, 0, 2).reshape(HEADS, TOKENS).astype(jnp.bfloat16)
    grad_conv_x = lax.optimization_barrier(jnp.sum(grad_wx.reshape(N_EXCH, NGROUPS, KCONV, group_width), axis=0)).transpose(1, 0, 2).reshape(KCONV, HEADS * HDIM)
    grad_conv_bc = lax.optimization_barrier(jnp.sum(grad_wbc.reshape(N_EXCH, NGROUPS, KCONV, pair_width), axis=0)).transpose(1, 0, 2).reshape(KCONV, NGROUPS * pair_width)
    grad_heads = jnp.stack([lax.optimization_barrier(jnp.sum(grad_bias.reshape(N_EXCH, HEADS), axis=0)), lax.optimization_barrier(jnp.sum(grad_decay.reshape(N_EXCH, HEADS), axis=0)), lax.optimization_barrier(jnp.sum(grad_skip.reshape(N_EXCH, HEADS), axis=0))])
    return (grad_x, grad_bc, grad_dt, grad_conv_x, grad_conv_bc, grad_heads)
```

```python
import functools

import jax
import jax.numpy as jnp
from jax import lax
from jax.experimental import pallas as pl
from jax.experimental.pallas import tpu as pltpu
from jax.sharding import PartitionSpec as P

DEV_GROUP = 8
GROUP = 1
MESH = pl.DeviceIdType.MESH
F32 = jnp.float32
BF16 = jnp.bfloat16


def nn(a, b):
    return lax.dot_general(a, b, (((1,), (0,)), ((), ())), preferred_element_type=F32)


def nt(a, b):
    return lax.dot_general(a, b, (((1,), (1,)), ((), ())), preferred_element_type=F32)


def split(a):
    high = a.astype(BF16)
    return high, (a - high.astype(F32)).astype(BF16)


def three(dot, a, b):
    return dot(a[0], b[0]) + (dot(a[0], b[1]) + dot(a[1], b[0]))


def iota(shape, dim):
    return lax.broadcasted_iota(jnp.int32, shape, dim)


def kernel(
    peers, slices, groups, *refs
):
    sources, refs = refs[:14], refs[14:]
    gx_ref, gbc_ref, gdt_ref, gwx_ref, gtaps_ref, gheads_ref = refs[:6]
    inputs, refs = refs[6:20], refs[20:]
    owner, lens, bias, a_log, skip, x_ref, bc_ref, dt_ref, cot_ref = inputs[:9]
    ssm_ref, cx_ref, cbc_ref, wx_ref, wbc_ref = inputs[9:]
    (
    msg, state, gath, msg_out, state_out, pad_x, pad_bc, dpx, dpbc, dw_ref, raw, back,
    fin, along_taps, across_taps,
    sem_in, sem_msg, sem_state, sem_gath, sem_along, sem_across, sem_back, sem_fin,
    ) = refs
    mine = lax.axis_index("exch")
    me = lax.axis_index("dp")
    depth, prompts, channels = cx_ref.shape
    taps_n = depth + 1
    responses = lens.shape[0]
    heads = bias.shape[0]
    width = channels // heads
    tokens = x_ref.shape[0]
    length = tokens // responses
    rows = bc_ref.shape[0]
    pair = cbc_ref.shape[2]
    half = pair // 2
    lanes = responses * heads
    base = 8 - depth

    def along(offset):
        return {"exch": lax.rem(mine + offset, peers)}

    def across(offset):
        return {"dp": lax.rem(me + offset, slices)}

    barrier = pltpu.get_barrier_semaphore()
    for offset in range(1, peers):
        pl.semaphore_signal(barrier, inc=1, device_id=along(offset), device_id_type=MESH)
    for offset in range(1, slices):
        pl.semaphore_signal(barrier, inc=1, device_id=across(offset), device_id_type=MESH)
    loads = [
        pltpu.make_async_copy(src, dst, sem_in.at[i])
        for i, (src, dst) in enumerate(zip(sources, inputs))
    ]
    sooner = (6, 0, 10, 11, 9)
    later = [i for i in range(len(loads)) if i not in sooner]
    for i in sooner:
        loads[i].start()
    for i in later:
        loads[i].start()
    for i in sooner[:-1]:
        loads[i].wait()
    tails = [
        jnp.concatenate([cx_ref[k].astype(F32), cbc_ref[k].astype(F32)], axis=1)
        for k in range(depth)
    ]

    def fill_msg(target, dst):
        small = [jnp.zeros((1, channels + pair), F32)] * depth
        flag = jnp.zeros((1, channels + pair), F32)
        for p in range(prompts):
            weight = (owner[p] == target).astype(F32)
            for k in range(depth):
                small[k] = small[k] + tails[k][p : p + 1] * weight
            flag = flag + weight
        dst[...] = jnp.concatenate(small + [flag], axis=0).astype(BF16)

    def fill_state(target, dst):
        big = jnp.zeros(ssm_ref.shape[1:], F32)
        for p in range(prompts):
            big = big + ssm_ref[p].astype(F32) * (owner[p] == target).astype(F32)
        dst[...] = big.astype(BF16)

    low = 1 - (2 * mine) // peers
    order = []
    for k in range(peers - 1):
        down = peers - 1 - k
        down = down - (mine - down + peers) // peers
        up = k + (k - mine + peers) // peers
        order.append(low * down + (1 - low) * up)

    for k in range(peers - 1):
        fill_msg(order[k], msg_out.at[k])
    fill_msg(mine, msg.at[mine])
    pl.semaphore_wait(barrier, slices - 1 + peers - 1)
    def remote(src, dst, sem, where):
        pltpu.make_async_remote_copy(
            src_ref=src,
            dst_ref=dst,
            send_sem=sem.at[0],
            recv_sem=sem.at[1],
            device_id=where,
            device_id_type=MESH,
        ).start()

    def settle(sem, which, ref):
        pltpu.make_async_copy(ref, ref, sem.at[which]).wait()

    def group_columns(ref, who):
        if groups == 1:
            return ref
        start = pl.multiple_of((who // DEV_GROUP) * pair, pair)
        return ref.at[:, pl.ds(start, pair)]

    for k in range(peers - 1):
        remote(msg_out.at[k], msg.at[mine], sem_msg, {"exch": order[k]})
    for o in range(1, slices):
        columns = group_columns(bc_ref, lax.rem(me + o, slices))
        remote(columns, gath.at[me], sem_gath, across(o))
    loads[sooner[-1]].wait()
    for k in range(peers - 1):
        fill_state(order[k], state_out.at[k])
        remote(state_out.at[k], state.at[mine], sem_state, {"exch": order[k]})
    fill_state(mine, state.at[mine])
    gath[me] = group_columns(bc_ref, me)[...]
    for i in later:
        loads[i].wait()
    row_head = lax.rem(iota((lanes, 1), 0), heads)

    def per_row(ref):
        out = jnp.zeros((lanes, 1), F32)
        for h in range(heads):
            out = jnp.where(row_head == h, ref[h], out)
        return out

    lane_head = iota((1, channels), 1) // width
    skip_row = jnp.zeros((1, channels), F32)
    for h in range(heads):
        skip_row = jnp.where(lane_head == h, skip[h], skip_row)
    dt_in = jnp.concatenate(
        [dt_ref[:, r * length : (r + 1) * length].astype(F32) for r in range(responses)], axis=0
    )
    dt_pre = dt_in + per_row(bias)
    small = jnp.exp(-jnp.abs(dt_pre))
    above = 1.0 + small
    log1p = jnp.where(above == 1.0, small, jnp.log(above) * (small / (above - 1.0)))
    dt = jnp.maximum(dt_pre, 0.0) + log1p
    rate = jnp.exp(per_row(a_log))
    first = iota((length, length), 0)
    second = iota((length, length), 1)
    upto = (first <= second).astype(F32)
    onward = (first >= second).astype(F32)
    causal = first <= second
    logs = lax.dot_general(
        -rate * dt,
        upto,
        (((1,), (0,)), ((), ())),
        preferred_element_type=F32,
        precision=lax.Precision.HIGHEST,
    )
    entry = jnp.exp(logs)
    logs_col = logs.T
    dt_col = dt.T
    entry_col = entry.T

    def spread_heads(cols, r):
        parts = [
            jnp.broadcast_to(cols[:, r * heads + h : r * heads + h + 1], (length, width))
            for h in range(heads)
        ]
        return jnp.concatenate(parts, axis=1)

    def indicator(r):
        row = iota((lanes, channels), 0)
        head = iota((lanes, channels), 1) // width
        return (row == r * heads + head).astype(BF16)

    for r in range(responses):
        block = slice(r * length, (r + 1) * length)
        pad_x[r, 8 : 8 + length] = x_ref[block].astype(F32)
    cots = []
    for r in range(responses):
        block = slice(r * length, (r + 1) * length)
        live = iota((length, 1), 0) < lens[r]
        cots.append(jnp.where(live, cot_ref[block].astype(F32), 0.0))
    settle(sem_msg, 1, msg.at[pl.ds(0, peers - 1)])
    got = [msg[z].astype(F32) for z in range(peers)]
    weights = [[None] * peers for _ in range(prompts)]
    seen = jnp.zeros((1, channels + pair), F32)
    for z in range(peers):
        present = got[z][depth : depth + 1]
        for j in range(prompts):
            weights[j][z] = jnp.where(seen == float(j), present, 0.0)
        seen = seen + present
    for r in range(responses):
        prev = jnp.zeros((depth, channels + pair), F32)
        for z in range(peers):
            prev = prev + got[z][0:depth] * weights[r // GROUP][z]
        pad_x[r, base:8] = prev[:, :channels]
        pad_bc[r, base:8] = prev[:, channels:]

    def convolve(pad, weight, r):
        pre = pad[r, base : base + length] * weight[0:1]
        for k in range(1, taps_n):
            pre = pre + pad[r, base + k : base + k + length] * weight[k : k + 1]
        gate = 1.0 / (1.0 + jnp.exp(-pre))
        return pre * gate, gate * (1.0 + pre * (1.0 - gate))

    wx = wx_ref[...]
    wbc = wbc_ref[...]
    x_acts = [convolve(pad_x, wx, r) for r in range(responses)]
    settle(sem_gath, 1, gath.at[pl.ds(0, slices - 1)])
    slots = length // rows
    for d in range(slices):
        r, place = d // slots, d % slots
        pad_bc[r, 8 + place * rows : 8 + (place + 1) * rows] = gath[d].astype(F32)
    bc_acts = [convolve(pad_bc, wbc, r) for r in range(responses)]
    across_rows = jnp.zeros((lanes, length), F32)
    dt_first = jnp.zeros((lanes, length), F32)
    row_index = iota((lanes, 1), 0)
    skip_sum = jnp.zeros((1, channels), F32)
    grad_wx = jnp.zeros((taps_n, channels), F32)
    b_grads, c_grads = [], []

    def weight_grad(grad, pad, r):
        parts = [
            jnp.sum(grad * pad[r, base + k : base + k + length], axis=0, keepdims=True)
            for k in range(taps_n)
        ]
        return jnp.concatenate(parts, axis=0)

    def input_grad(ref, weight, r):
        total = ref[r, depth : depth + length] * weight[0:1]
        for k in range(1, taps_n):
            total = total + ref[r, depth - k : depth - k + length] * weight[k : k + 1]
        return total

    for r in range(responses):
        act, slope = x_acts[r]
        cot = cots[r]
        cot_b = cot.astype(BF16)
        dt_full = spread_heads(dt_col, r)
        weighted = split(act * dt_full)
        proj_b = split(bc_acts[r][0][:, :half])
        proj_c = split(bc_acts[r][0][:, half:])
        scores = three(nt, proj_b, proj_c)
        score_grad = jnp.zeros((length, length), F32)
        for h in range(heads):
            i = r * heads + h
            cols = slice(h * width, (h + 1) * width)
            cot_h = cot_b[:, cols]
            gap = logs[i : i + 1] - logs_col[:, i : i + 1]
            decay = jnp.where(causal, jnp.exp(jnp.where(causal, gap, 0.0)), 0.0)
            mix = scores * decay
            mix_grad = nt(weighted[0][:, cols], cot_h) + nt(weighted[1][:, cols], cot_h)
            high, low = split(mix)
            dw_ref[r, :, cols] = nn(high, cot_h) + nn(low, cot_h)
            score_grad = score_grad + mix_grad * decay
            found = jnp.sum(mix_grad * mix, axis=0, keepdims=True)
            across_rows = jnp.where(row_index == i, found, across_rows)
        dw = dw_ref[r]
        prod = split(dw * act)
        mark = indicator(r)
        dt_first = dt_first + (nt(mark, prod[0]) + nt(mark, prod[1]))
        skip_sum = skip_sum + jnp.sum(cot * act, axis=0, keepdims=True)
        pre_grad = (dw * dt_full + skip_row * cot) * slope
        dpx[r, 0:length] = pre_grad
        dpx[r, length : length + 8] = jnp.zeros((8, channels), F32)
        grad_wx = grad_wx + weight_grad(pre_grad, pad_x, r)
        gx_ref[r * length : (r + 1) * length] = input_grad(dpx, wx, r).astype(BF16)
        b_grads.append(three(nn, split(score_grad), proj_c))
        c_grads.append(three(nn, split(score_grad.T), proj_b))
    settle(sem_state, 1, state.at[pl.ds(0, peers - 1)])
    starts = []
    grad_taps = jnp.zeros((taps_n, pair), F32)
    for r in range(responses):
        start = jnp.zeros(state.shape[1:], F32)
        for z in range(peers):
            pick = weights[r // GROUP][z][:, : state.shape[2]]
            start = start + state[z].astype(F32) * pick
        start = start.astype(BF16)
        starts.append(start)
        fed = split(cots[r] * spread_heads(entry_col, r))
        c_grad = c_grads[r] + (nn(fed[0], start) + nn(fed[1], start))
        slope = bc_acts[r][1]
        pre_grad = jnp.concatenate([b_grads[r], c_grad], axis=1) * slope
        dpbc[r, 0:length] = pre_grad
        dpbc[r, length : length + 8] = jnp.zeros((8, pair), F32)
        grad_taps = grad_taps + weight_grad(pre_grad, pad_bc, r)
    along_taps[mine] = jnp.concatenate([grad_taps[:, :half], grad_taps[:, half:]], axis=0)
    for o in range(1, peers):
        remote(along_taps.at[mine], along_taps.at[mine], sem_along, along(o))
    for r in range(responses):
        block = input_grad(dpbc, wbc, r)
        for place in range(slots):
            raw[r * slots + place] = block[place * rows : (place + 1) * rows]
    for o in range(1, slices):
        remote(raw.at[lax.rem(me + o, slices)], back.at[me], sem_back, across(o))
    back[me] = raw[me]
    entry_grad = jnp.zeros((lanes, length), F32)
    for r in range(responses):
        proj_c = split(bc_acts[r][0][:, half:])
        carried = nt(proj_c[0], starts[r]) + nt(proj_c[1], starts[r])
        prod = split(carried * cots[r])
        mark = indicator(r)
        entry_grad = entry_grad + (nt(mark, prod[0]) + nt(mark, prod[1]))
    log_grad = across_rows + entry * entry_grad - dt * dt_first
    step_grad = lax.dot_general(
        log_grad,
        onward,
        (((1,), (0,)), ((), ())),
        preferred_element_type=F32,
        precision=lax.Precision.HIGHEST,
    )
    dt_grad = dt_first - rate * step_grad
    raw_grad = dt_grad * (1.0 / (1.0 + jnp.exp(-dt_pre)))
    for r in range(responses):
        gdt_ref[:, r * length : (r + 1) * length] = raw_grad[
            r * heads : (r + 1) * heads
        ].astype(BF16)
    bias_rows = jnp.sum(raw_grad, axis=1, keepdims=True)
    decay_rows = -rate * jnp.sum(dt * step_grad, axis=1, keepdims=True)
    bias_grad = jnp.zeros((heads, 1), F32)
    decay_grad = jnp.zeros((heads, 1), F32)
    for r in range(responses):
        bias_grad = bias_grad + bias_rows[r * heads : (r + 1) * heads]
        decay_grad = decay_grad + decay_rows[r * heads : (r + 1) * heads]
    own = iota((heads, channels), 0) == iota((heads, channels), 1) // width
    skip_grad = jnp.sum(jnp.where(own, skip_sum, 0.0), axis=1, keepdims=True)
    column = iota((heads, half), 1)
    head_block = jnp.where(
        column == 0,
        bias_grad,
        jnp.where(column == 1, decay_grad, jnp.where(column == 2, skip_grad, 0.0)),
    )
    fin[mine] = jnp.zeros(fin.shape[1:], F32)
    fin[mine, 0:taps_n, 0:channels] = grad_wx
    fin[mine, taps_n : taps_n + heads, 0:half] = head_block
    for o in range(1, peers):
        remote(fin.at[mine], fin.at[mine], sem_fin, along(o))
    settle(sem_along, 1, along_taps.at[pl.ds(0, peers - 1)])
    total = along_taps[0]
    for z in range(1, peers):
        total = total + along_taps[z]
    across_taps[me] = total
    for o in range(1, slices):
        remote(across_taps.at[me], across_taps.at[me], sem_across, across(o))
    settle(sem_back, 1, back.at[pl.ds(0, slices - 1)])
    for q in range(groups):
        total = back[q * DEV_GROUP]
        for d in range(1, DEV_GROUP):
            total = total + back[q * DEV_GROUP + d]
        gbc_ref[:, q * pair : (q + 1) * pair] = total.astype(BF16)
    settle(sem_fin, 1, fin.at[pl.ds(0, peers - 1)])
    total = fin[0]
    for z in range(1, peers):
        total = total + fin[z]
    gwx_ref[...] = total[0:taps_n, 0:channels]
    gheads_ref[...] = total[:, 0:half].T[0:3, taps_n : taps_n + heads]

    for sem, ref in (
        (sem_msg, msg_out.at[pl.ds(0, peers - 1)]),
        (sem_gath, gath.at[pl.ds(0, slices - 1)]),
        (sem_state, state_out.at[pl.ds(0, peers - 1)]),
        (sem_along, along_taps.at[pl.ds(0, peers - 1)]),
        (sem_back, raw.at[pl.ds(0, slices - 1)]),
        (sem_fin, fin.at[pl.ds(0, peers - 1)]),
    ):
        settle(sem, 0, ref)
    settle(sem_across, 1, across_taps.at[pl.ds(0, slices - 1)])
    for q in range(groups):
        total = across_taps[q * DEV_GROUP]
        for d in range(1, DEV_GROUP):
            total = total + across_taps[q * DEV_GROUP + d]
        gtaps_ref[:, q * pair : q * pair + half] = total[0:taps_n]
        gtaps_ref[:, q * pair + half : (q + 1) * pair] = total[taps_n:]
    settle(sem_across, 0, across_taps.at[pl.ds(0, slices - 1)])


def finish(*refs):
    count = len(refs) // 2
    sems = refs[-1]
    copies = [
        pltpu.make_async_copy(src, dst, sems.at[i])
        for i, (src, dst) in enumerate(zip(refs[:count], refs[count:-1]))
    ]
    for copy in copies:
        copy.start()
    for copy in copies:
        copy.wait()


def local(
    x_raw, bc_raw, dt_raw, cotangent, ssm_state, conv_x_state, conv_bc_state, owner, resp_len,
    conv_x_weight, conv_bc_weight, dt_bias, a_log, skip_d,
):
    peers = lax.axis_size("exch")
    slices = lax.axis_size("dp")
    prompts, heads, width, nstate = ssm_state.shape
    channels = x_raw.shape[1]
    pair = 2 * nstate
    depth = conv_x_state.shape[1]
    responses = resp_len.shape[0]
    tokens = x_raw.shape[0]
    length = tokens // responses
    rows, all_pairs = bc_raw.shape
    groups = all_pairs // pair
    bc_state, bc_weight = conv_bc_state, conv_bc_weight
    if groups > 1:
        first = (lax.axis_index("dp") // DEV_GROUP) * pair
        bc_state = lax.dynamic_slice_in_dim(conv_bc_state, first, pair, 2)
        bc_weight = lax.dynamic_slice_in_dim(conv_bc_weight, first, pair, 1)
    ssm = ssm_state.reshape(prompts, heads * width, nstate)
    rows_fin = -(-(depth + 1 + heads) // 8) * 8
    vmem = pl.BlockSpec(memory_space=pltpu.VMEM)
    dma = pltpu.SemaphoreType.DMA
    outs = (
        jax.ShapeDtypeStruct((tokens, channels), BF16),
        jax.ShapeDtypeStruct((rows, all_pairs), BF16),
        jax.ShapeDtypeStruct((heads, tokens), BF16),
        jax.ShapeDtypeStruct((depth + 1, channels), F32),
        jax.ShapeDtypeStruct((depth + 1, all_pairs), F32),
        jax.ShapeDtypeStruct((3, heads), F32),
    )
    staged = tuple(pltpu.VMEM(out.shape, out.dtype) for out in outs)
    args = (
        owner, resp_len, dt_bias, a_log, skip_d, x_raw, bc_raw, dt_raw, cotangent, ssm,
        conv_x_state.transpose(1, 0, 2), bc_state.transpose(1, 0, 2), conv_x_weight, bc_weight,
    )
    held = pl.pallas_call(
        functools.partial(kernel, peers, slices, groups),
        out_shape=staged,
        in_specs=[pl.BlockSpec(memory_space=pltpu.HBM)] * 14,
        out_specs=[vmem] * 6,
        scratch_shapes=[pltpu.SMEM(a.shape, a.dtype) for a in args[:5]]
        + [pltpu.VMEM(a.shape, a.dtype) for a in args[5:]]
        + [
            pltpu.VMEM((peers, depth + 1, channels + pair), BF16),
            pltpu.VMEM((peers, heads * width, nstate), BF16),
            pltpu.VMEM((slices, rows, pair), BF16),
            pltpu.VMEM((peers, depth + 1, channels + pair), BF16),
            pltpu.VMEM((peers, heads * width, nstate), BF16),
            pltpu.VMEM((responses, length + 8, channels), F32),
            pltpu.VMEM((responses, length + 8, pair), F32),
            pltpu.VMEM((responses, length + 8, channels), F32),
            pltpu.VMEM((responses, length + 8, pair), F32),
            pltpu.VMEM((responses, length, channels), F32),
            pltpu.VMEM((slices, rows, pair), F32),
            pltpu.VMEM((slices, rows, pair), F32),
            pltpu.VMEM((peers, rows_fin, max(channels, nstate)), F32),
            pltpu.VMEM((peers, 2 * depth + 2, nstate), F32),
            pltpu.VMEM((slices, 2 * depth + 2, nstate), F32),
            dma((14,)),
        ]
        + [dma((2,))] * 7,
        compiler_params=pltpu.CompilerParams(
            collective_id=0, has_side_effects=True
        ),
    )(*args)
    anywhere = pl.BlockSpec(memory_space=pl.ANY)
    return pl.pallas_call(
        finish,
        out_shape=outs,
        in_specs=[vmem] * 6,
        out_specs=[anywhere] * 6,
        scratch_shapes=[dma((6,))],
        compiler_params=pltpu.CompilerParams(vmem_limit_bytes=16 * 1024 * 1024),
    )(*held)


def solution(mesh):
    in_specs = (
        P("exch", "dp"),
        P(("exch", "dp"), None),
        P("dp", "exch"),
        P("exch", "dp"),
        P("exch", "dp", None, None),
        P("exch", None, "dp"),
        P("exch", None, None),
        P("exch"),
        P("exch"),
        P(None, "dp"),
        P(),
        P("dp"),
        P("dp"),
        P("dp"),
    )
    out_specs = (
        P("exch", "dp"),
        P(("exch", "dp"), None),
        P("dp", "exch"),
        P(None, "dp"),
        P(),
        P(None, "dp"),
    )
    return jax.shard_map(local, mesh=mesh, in_specs=in_specs, out_specs=out_specs, check_vma=False)
```

```python
import functools

import jax
import jax.numpy as jnp
from jax import lax
from jax.experimental import pallas as pl
from jax.experimental.pallas import tpu as pltpu
from jax.sharding import PartitionSpec as P

DEV_GROUP = 8
FIRST = 2
GROUP = 1
MESH = pl.DeviceIdType.MESH
F32 = jnp.float32
BF16 = jnp.bfloat16


def nn(a, b):
    return lax.dot_general(a, b, (((1,), (0,)), ((), ())), preferred_element_type=F32)


def nt(a, b):
    return lax.dot_general(a, b, (((1,), (1,)), ((), ())), preferred_element_type=F32)


def split(a):
    high = a.astype(BF16)
    return high, (a - high.astype(F32)).astype(BF16)


def three(dot, a, b):
    return dot(a[0], b[0]) + (dot(a[0], b[1]) + dot(a[1], b[0]))


def iota(shape, dim):
    return lax.broadcasted_iota(jnp.int32, shape, dim)


def is_direct(peers, slices, groups):
    return groups == 1 and peers > 1 and FIRST < slices and peers * slices <= 64


def kernel(
    peers, slices, groups, *refs
):
    sources, refs = refs[:14], refs[14:]
    gx_ref, gbc_ref, gdt_ref, gwx_ref, gtaps_ref, gheads_ref = refs[:6]
    inputs, refs = refs[6:20], refs[20:]
    owner, lens, bias, a_log, skip, x_ref, bc_ref, dt_ref, cot_ref = inputs[:9]
    ssm_ref, cx_ref, cbc_ref, wx_ref, wbc_ref = inputs[9:]
    (
    msg, state, gath, msg_out, state_out, pad_x, pad_bc, dpx, dpbc, dw_ref, raw, back,
    fin, all_taps, across_taps, sum_taps, x_act, x_slope, bc_slope, tap_rows, decays, products, score_grads, fed,
    sem_in, sem_msg, sem_state, sem_gath, sem_along, sem_across, sem_back, sem_fin,
    ) = refs
    mine = lax.axis_index("exch")
    me = lax.axis_index("dp")
    depth, prompts, channels = cx_ref.shape
    taps_n = depth + 1
    responses = lens.shape[0]
    heads = bias.shape[0]
    width = channels // heads
    tokens = x_ref.shape[0]
    length = tokens // responses
    rows = bc_ref.shape[0]
    pair = cbc_ref.shape[2]
    half = pair // 2
    lanes = responses * heads
    base = 8 - depth

    def along(offset):
        return {"exch": lax.rem(mine + offset, peers)}

    def spot(place):
        return {"dp": place % slices, "exch": place // slices}

    def add_up(terms):
        while len(terms) > 1:
            terms = [sum(terms[i + 1 : i + 2], terms[i]) for i in range(0, len(terms), 2)]
        return terms[0]

    devices = peers * slices
    direct = is_direct(peers, slices, groups)

    def across(offset):
        return {"dp": lax.rem(me + offset, slices)}

    barrier = pltpu.get_barrier_semaphore()
    for offset in range(1, peers):
        pl.semaphore_signal(barrier, inc=1, device_id=along(offset), device_id_type=MESH)
    for offset in range(1, slices):
        pl.semaphore_signal(barrier, inc=1, device_id=across(offset), device_id_type=MESH)
    loads = [
        pltpu.make_async_copy(src, dst, sem_in.at[i])
        for i, (src, dst) in enumerate(zip(sources, inputs))
    ]
    sooner = (6, 0, 10, 11, 9)
    later = [i for i in range(len(loads)) if i not in sooner]
    for i in sooner:
        loads[i].start()
    for i in later:
        loads[i].start()
    for i in sooner[:-1]:
        loads[i].wait()
    tails = [
        jnp.concatenate([cx_ref[k].astype(F32), cbc_ref[k].astype(F32)], axis=1)
        for k in range(depth)
    ]

    def fill_msg(target, dst):
        small = [jnp.zeros((1, channels + pair), F32)] * depth
        flag = jnp.zeros((1, channels + pair), F32)
        for p in range(prompts):
            weight = (owner[p] == target).astype(F32)
            for k in range(depth):
                small[k] = small[k] + tails[k][p : p + 1] * weight
            flag = flag + weight
        dst[...] = jnp.concatenate(small + [flag], axis=0).astype(BF16)

    def fill_state(target, dst):
        big = jnp.zeros(ssm_ref.shape[1:], F32)
        for p in range(prompts):
            big = big + ssm_ref[p].astype(F32) * (owner[p] == target).astype(F32)
        dst[...] = big.astype(BF16)

    low = 1 - (2 * mine) // peers
    order = []
    for k in range(peers - 1):
        down = peers - 1 - k
        down = down - (mine - down + peers) // peers
        up = k + (k - mine + peers) // peers
        order.append(low * down + (1 - low) * up)

    for k in range(peers - 1):
        fill_msg(order[k], msg_out.at[k])
    fill_msg(mine, msg.at[mine])
    pl.semaphore_wait(barrier, slices - 1 + peers - 1)
    def remote(src, dst, sem, where):
        pltpu.make_async_remote_copy(
            src_ref=src,
            dst_ref=dst,
            send_sem=sem.at[0],
            recv_sem=sem.at[1],
            device_id=where,
            device_id_type=MESH,
        ).start()

    def settle(sem, which, ref):
        pltpu.make_async_copy(ref, ref, sem.at[which]).wait()

    def group_columns(ref, who):
        if groups == 1:
            return ref
        start = pl.multiple_of((who // DEV_GROUP) * pair, pair)
        return ref.at[:, pl.ds(start, pair)]

    for k in range(peers - 1):
        remote(msg_out.at[k], msg.at[mine], sem_msg, {"exch": order[k]})
    for o in range(1, slices):
        columns = group_columns(bc_ref, lax.rem(me + o, slices))
        remote(columns, gath.at[me], sem_gath, across(o))
    loads[sooner[-1]].wait()
    for k in range(peers - 1):
        fill_state(order[k], state_out.at[k])
        remote(state_out.at[k], state.at[mine], sem_state, {"exch": order[k]})
    fill_state(mine, state.at[mine])
    gath[me] = group_columns(bc_ref, me)[...]
    for i in later:
        loads[i].wait()
    row_head = lax.rem(iota((lanes, 1), 0), heads)

    def per_row(ref):
        out = jnp.zeros((lanes, 1), F32)
        for h in range(heads):
            out = jnp.where(row_head == h, ref[h], out)
        return out

    lane_head = iota((1, channels), 1) // width
    skip_row = jnp.zeros((1, channels), F32)
    for h in range(heads):
        skip_row = jnp.where(lane_head == h, skip[h], skip_row)
    dt_in = jnp.concatenate(
        [dt_ref[:, r * length : (r + 1) * length].astype(F32) for r in range(responses)], axis=0
    )
    dt_pre = dt_in + per_row(bias)
    small = jnp.exp(-jnp.abs(dt_pre))
    above = 1.0 + small
    log1p = jnp.where(above == 1.0, small, jnp.log(above) * (small / (above - 1.0)))
    dt = jnp.maximum(dt_pre, 0.0) + log1p
    rate = jnp.exp(per_row(a_log))
    first = iota((length, length), 0)
    second = iota((length, length), 1)
    upto = (first <= second).astype(BF16)
    onward = (first >= second).astype(BF16)
    causal = first <= second

    def running(rows_in, ones):
        high = rows_in.astype(BF16).astype(F32)
        rest = rows_in - high
        middle = rest.astype(BF16).astype(F32)
        parts = nn(jnp.concatenate([high, middle, rest - middle], axis=0).astype(BF16), ones)
        return parts[:lanes] + (parts[lanes : 2 * lanes] + parts[2 * lanes :])

    logs = running(-rate * dt, upto)
    entry = jnp.exp(logs)
    logs_col = logs.T
    dt_col = dt.T
    entry_col = entry.T

    def spread_heads(cols, r):
        parts = [
            jnp.broadcast_to(cols[:, r * heads + h : r * heads + h + 1], (length, width))
            for h in range(heads)
        ]
        return jnp.concatenate(parts, axis=1)

    def indicator(r):
        row = iota((lanes, channels), 0)
        head = iota((lanes, channels), 1) // width
        return (row == r * heads + head).astype(BF16)

    wx = wx_ref[...]
    wbc = wbc_ref[...]

    def convolve(pad, weight, r, count):
        pre = pad[r, base : base + count] * weight[0:1]
        for k in range(1, taps_n):
            pre = pre + pad[r, base + k : base + k + count] * weight[k : k + 1]
        gate = 1.0 / (1.0 + jnp.exp(-pre))
        return pre * gate, gate * (1.0 + pre * (1.0 - gate))

    cots, cots_b, dt_fulls = [], [], []
    for r in range(responses):
        block = slice(r * length, (r + 1) * length)
        pad_x[r, 0:8] = jnp.zeros((8, channels), F32)
        pad_x[r, 8 : 8 + length] = x_ref[block].astype(F32)
        live = iota((length, 1), 0) < lens[r]
        cots.append(jnp.where(live, cot_ref[block].astype(F32), 0.0))
        cots_b.append(cots[r].astype(BF16))
        dt_fulls.append(spread_heads(dt_col, r))
        x_act[r], x_slope[r] = convolve(pad_x, wx, r, length)
        weighted = split(x_act[r] * dt_fulls[r])
        total = jnp.zeros((length, length), F32)
        for h in range(heads):
            i = r * heads + h
            cols = slice(h * width, (h + 1) * width)
            gap = logs[i : i + 1] - logs_col[:, i : i + 1]
            decay = jnp.where(causal, jnp.exp(jnp.where(causal, gap, 0.0)), 0.0)
            cot_h = cots_b[r][:, cols]
            product = (nt(weighted[0][:, cols], cot_h) + nt(weighted[1][:, cols], cot_h)) * decay
            decays[r, h] = decay
            products[r, h] = product
            total = total + product
        score_grads[r] = total
        fed[r, 0], fed[r, 1] = split(cots[r] * spread_heads(entry_col, r))
    settle(sem_msg, 1, msg.at[pl.ds(0, peers - 1)])
    got = [msg[z].astype(F32) for z in range(peers)]
    weights = [[None] * peers for _ in range(prompts)]
    seen = jnp.zeros((1, channels + pair), F32)
    for z in range(peers):
        present = got[z][depth : depth + 1]
        for j in range(prompts):
            weights[j][z] = jnp.where(seen == float(j), present, 0.0)
        seen = seen + present
    for r in range(responses):
        prev = jnp.zeros((depth, channels + pair), F32)
        for z in range(peers):
            prev = prev + got[z][0:depth] * weights[r // GROUP][z]
        pad_x[r, base:8] = prev[:, :channels]
        pad_bc[r, base:8] = prev[:, channels:]

    grads, grads_t = [], []
    for r in range(responses):
        act, slope = convolve(pad_x, wx, r, 8)
        x_act[r, 0:8] = act
        x_slope[r, 0:8] = slope
        scaled = act * dt_fulls[r][0:8]
        high = scaled.astype(BF16).astype(F32)
        stack = [
            jnp.where(lane_head == h, part, 0.0)
            for part in (high, scaled - high)
            for h in range(heads)
        ]
        both = nt(jnp.concatenate(stack, axis=0).astype(BF16), cots_b[r])
        total = jnp.zeros((8, length), F32)
        for h in range(heads):
            lower = 8 * (heads + h)
            product = (both[8 * h : 8 * h + 8] + both[lower : lower + 8]) * decays[r, h, 0:8]
            products[r, h, 0:8] = product
            total = total + product
        score_grads[r, 0:8] = total
        whole = score_grads[r]
        grads.append(split(whole))
        grads_t.append(split(whole.T))
    settle(sem_gath, 1, gath.at[pl.ds(0, slices - 1)])
    slots = length // rows
    for d in range(slices):
        r, place = d // slots, d % slots
        pad_bc[r, 8 + place * rows : 8 + (place + 1) * rows] = gath[d].astype(F32)

    def weight_grad(grad, pad, r):
        parts = [
            jnp.sum(grad * pad[r, base + k : base + k + length], axis=0, keepdims=True)
            for k in range(taps_n)
        ]
        return jnp.concatenate(parts, axis=0)

    def input_grad(ref, weight, r):
        total = ref[r, depth : depth + length] * weight[0:1]
        for k in range(1, taps_n):
            total = total + ref[r, depth - k : depth - k + length] * weight[k : k + 1]
        return total

    projs = []
    grad_taps = jnp.zeros((taps_n, pair), F32)
    for r in range(responses):
        act, slope = convolve(pad_bc, wbc, r, length)
        proj_b, proj_c = split(act[:, :half]), split(act[:, half:])
        projs.append((proj_b, proj_c))
        b_grad = three(nn, grads[r], proj_c)
        c_grad = three(nn, grads_t[r], proj_b)
        pre_grad = jnp.concatenate([b_grad, c_grad], axis=1) * slope
        dpbc[r, 0:length] = pre_grad
        dpbc[r, length : length + 8] = jnp.zeros((8, pair), F32)
        grad_taps = grad_taps + weight_grad(pre_grad, pad_bc, r)
        bc_slope[r] = slope[:, half:]
        for k in range(taps_n):
            window = pad_bc[r, base + k : base + k + length, half:]
            tap_rows[r, k] = slope[:, half:] * window
    across_rows = jnp.zeros((lanes, length), F32)
    dt_first = jnp.zeros((lanes, length), F32)
    row_index = iota((lanes, 1), 0)
    skip_sum = jnp.zeros((1, channels), F32)
    grad_wx = jnp.zeros((taps_n, channels), F32)
    def local_rows(r, found_rows, dt_rows, skip_row_sum, taps_x):
        proj_b, proj_c = projs[r]
        scores = three(nt, proj_b, proj_c)
        for h in range(heads):
            i = r * heads + h
            cols = slice(h * width, (h + 1) * width)
            cot_h = cots_b[r][:, cols]
            high, low = split(scores * decays[r, h])
            dw_ref[r, :, cols] = nn(high, cot_h) + nn(low, cot_h)
            found = jnp.sum(scores * products[r, h], axis=0, keepdims=True)
            found_rows = jnp.where(row_index == i, found, found_rows)
        act, dw = x_act[r], dw_ref[r]
        prod = split(dw * act)
        mark = indicator(r)
        dt_rows = dt_rows + (nt(mark, prod[0]) + nt(mark, prod[1]))
        skip_row_sum = skip_row_sum + jnp.sum(cots[r] * act, axis=0, keepdims=True)
        pre_grad = (dw * dt_fulls[r] + skip_row * cots[r]) * x_slope[r]
        dpx[r, 0:length] = pre_grad
        dpx[r, length : length + 8] = jnp.zeros((8, channels), F32)
        taps_x = taps_x + weight_grad(pre_grad, pad_x, r)
        gx_ref[r * length : (r + 1) * length] = input_grad(dpx, wx, r).astype(BF16)
        return found_rows, dt_rows, skip_row_sum, taps_x

    sums = (across_rows, dt_first, skip_sum, grad_wx)
    early = responses
    for r in range(early):
        sums = local_rows(r, *sums)
    settle(sem_state, 1, state.at[pl.ds(0, peers - 1)])
    starts, lates = [], []
    for r in range(responses):
        start = jnp.zeros(state.shape[1:], BF16)
        for z in range(peers):
            pick = weights[r // GROUP][z][:, : state.shape[2]].astype(BF16)
            start = start + state[z] * pick
        starts.append(start)
        late = nn(fed[r, 0], start) + nn(fed[r, 1], start)
        lates.append(late)
        more = jnp.concatenate(
            [jnp.sum(late * tap_rows[r, k], axis=0, keepdims=True) for k in range(taps_n)], axis=0
        )
        grad_taps = grad_taps + jnp.concatenate([jnp.zeros_like(more), more], axis=1)
    packed = jnp.concatenate([grad_taps[:, :half], grad_taps[:, half:]], axis=0)
    if direct:
        place = mine * slices + me
        helper = slices + 1
        is_helper = place == helper
        is_first = place < FIRST
        all_taps[place] = packed
        for target in (*range(FIRST), helper):

            @pl.when(place != target)
            def _():
                remote(all_taps.at[place], all_taps.at[place], sem_along, spot(target))

        def sum_all():
            settle(sem_along, 1, all_taps.at[pl.ds(0, devices - 1)])
            for q in range(groups):
                sum_taps[q] = add_up(
                    [
                        all_taps[z * slices + q * DEV_GROUP + d]
                        for z in range(peers)
                        for d in range(DEV_GROUP)
                    ]
                )

    else:
        all_taps[mine] = packed
        for o in range(1, peers):
            remote(all_taps.at[mine], all_taps.at[mine], sem_along, along(o))
    for r in range(responses):
        dpbc[r, 0:length, half:] = dpbc[r, 0:length, half:] + lates[r] * bc_slope[r]
        block = input_grad(dpbc, wbc, r)
        for place in range(slots):
            raw[r * slots + place] = block[place * rows : (place + 1) * rows]
    for o in range(1, slices):
        remote(raw.at[lax.rem(me + o, slices)], back.at[me], sem_back, across(o))
    back[me] = raw[me]
    for r in range(early, responses):
        sums = local_rows(r, *sums)
    across_rows, dt_first, skip_sum, grad_wx = sums
    entry_grad = jnp.zeros((lanes, length), F32)
    for r in range(responses):
        proj_c = projs[r][1]
        carried = nt(proj_c[0], starts[r]) + nt(proj_c[1], starts[r])
        prod = split(carried * cots[r])
        mark = indicator(r)
        entry_grad = entry_grad + (nt(mark, prod[0]) + nt(mark, prod[1]))
    log_grad = across_rows + entry * entry_grad - dt * dt_first
    step_grad = running(log_grad, onward)
    dt_grad = dt_first - rate * step_grad
    raw_grad = dt_grad * (1.0 / (1.0 + jnp.exp(-dt_pre)))
    for r in range(responses):
        gdt_ref[:, r * length : (r + 1) * length] = raw_grad[
            r * heads : (r + 1) * heads
        ].astype(BF16)
    bias_rows = jnp.sum(raw_grad, axis=1, keepdims=True)
    decay_rows = -rate * jnp.sum(dt * step_grad, axis=1, keepdims=True)
    bias_grad = jnp.zeros((heads, 1), F32)
    decay_grad = jnp.zeros((heads, 1), F32)
    for r in range(responses):
        bias_grad = bias_grad + bias_rows[r * heads : (r + 1) * heads]
        decay_grad = decay_grad + decay_rows[r * heads : (r + 1) * heads]
    own = iota((heads, channels), 0) == iota((heads, channels), 1) // width
    skip_grad = jnp.sum(jnp.where(own, skip_sum, 0.0), axis=1, keepdims=True)
    at_head = iota((heads, half), 0) == iota((heads, half), 1)
    fin[mine] = jnp.zeros(fin.shape[1:], F32)
    fin[mine, 0:taps_n, 0:channels] = grad_wx
    for i, grad in enumerate((bias_grad, decay_grad, skip_grad)):
        row = jnp.sum(jnp.where(at_head, grad, 0.0), axis=0, keepdims=True)
        fin[mine, taps_n + i : taps_n + i + 1, 0:half] = row
    for o in range(1, peers):
        remote(fin.at[mine], fin.at[mine], sem_fin, along(o))
    if direct:

        @pl.when(is_helper)
        def _():
            sum_all()
            for k in range(FIRST, devices):
                if k != helper:
                    remote(sum_taps, sum_taps, sem_across, spot(k))
    else:
        settle(sem_along, 1, all_taps.at[pl.ds(0, peers - 1)])
        across_taps[me] = add_up([all_taps[z] for z in range(peers)])
        for o in range(1, slices):
            remote(across_taps.at[me], across_taps.at[me], sem_across, across(o))
    settle(sem_back, 1, back.at[pl.ds(0, slices - 1)])
    for q in range(groups):
        total = back[q * DEV_GROUP]
        for d in range(1, DEV_GROUP):
            total = total + back[q * DEV_GROUP + d]
        gbc_ref[:, q * pair : (q + 1) * pair] = total.astype(BF16)
    settle(sem_fin, 1, fin.at[pl.ds(0, peers - 1)])
    total = fin[0]
    for z in range(1, peers):
        total = total + fin[z]
    gwx_ref[...] = total[0:taps_n, 0:channels]
    gheads_ref[...] = total[taps_n : taps_n + 3, 0:heads]

    for sem, ref in (
        (sem_msg, msg_out.at[pl.ds(0, peers - 1)]),
        (sem_gath, gath.at[pl.ds(0, slices - 1)]),
        (sem_state, state_out.at[pl.ds(0, peers - 1)]),
        (sem_back, raw.at[pl.ds(0, slices - 1)]),
        (sem_fin, fin.at[pl.ds(0, peers - 1)]),
    ):
        settle(sem, 0, ref)
    if direct:

        @pl.when(is_helper)
        def _():
            settle(sem_along, 0, all_taps.at[pl.ds(0, FIRST)])
            settle(sem_across, 0, all_taps.at[pl.ds(0, (devices - 1 - FIRST) * groups)])

        @pl.when(is_first)
        def _():
            settle(sem_along, 0, all_taps.at[pl.ds(0, FIRST)])
            sum_all()

        @pl.when(jnp.logical_not(jnp.logical_or(is_first, is_helper)))
        def _():
            settle(sem_along, 0, all_taps.at[pl.ds(0, FIRST + 1)])
            settle(sem_across, 1, sum_taps)
    else:
        settle(sem_along, 0, all_taps.at[pl.ds(0, peers - 1)])
        settle(sem_across, 0, across_taps.at[pl.ds(0, slices - 1)])
        settle(sem_across, 1, across_taps.at[pl.ds(0, slices - 1)])
        for q in range(groups):
            sum_taps[q] = add_up([across_taps[q * DEV_GROUP + d] for d in range(DEV_GROUP)])
    for q in range(groups):
        total = sum_taps[q]
        gtaps_ref[:, q * pair : q * pair + half] = total[0:taps_n]
        gtaps_ref[:, q * pair + half : (q + 1) * pair] = total[taps_n:]


def finish(*refs):
    count = len(refs) // 2
    sems = refs[-1]
    copies = [
        pltpu.make_async_copy(src, dst, sems.at[i])
        for i, (src, dst) in enumerate(zip(refs[:count], refs[count:-1]))
    ]
    for copy in copies:
        copy.start()
    for copy in copies:
        copy.wait()


def local(
    x_raw, bc_raw, dt_raw, cotangent, ssm_state, conv_x_state, conv_bc_state, owner, resp_len,
    conv_x_weight, conv_bc_weight, dt_bias, a_log, skip_d,
):
    peers = lax.axis_size("exch")
    slices = lax.axis_size("dp")
    prompts, heads, width, nstate = ssm_state.shape
    channels = x_raw.shape[1]
    pair = 2 * nstate
    depth = conv_x_state.shape[1]
    responses = resp_len.shape[0]
    tokens = x_raw.shape[0]
    length = tokens // responses
    rows, all_pairs = bc_raw.shape
    groups = all_pairs // pair
    bc_state, bc_weight = conv_bc_state, conv_bc_weight
    if groups > 1:
        first = (lax.axis_index("dp") // DEV_GROUP) * pair
        bc_state = lax.dynamic_slice_in_dim(conv_bc_state, first, pair, 2)
        bc_weight = lax.dynamic_slice_in_dim(conv_bc_weight, first, pair, 1)
    ssm = ssm_state.reshape(prompts, heads * width, nstate)
    senders = peers * slices if is_direct(peers, slices, groups) else peers
    rows_fin = -(-(depth + 4) // 8) * 8
    vmem = pl.BlockSpec(memory_space=pltpu.VMEM)
    dma = pltpu.SemaphoreType.DMA
    outs = (
        jax.ShapeDtypeStruct((tokens, channels), BF16),
        jax.ShapeDtypeStruct((rows, all_pairs), BF16),
        jax.ShapeDtypeStruct((heads, tokens), BF16),
        jax.ShapeDtypeStruct((depth + 1, channels), F32),
        jax.ShapeDtypeStruct((depth + 1, all_pairs), F32),
        jax.ShapeDtypeStruct((3, heads), F32),
    )
    staged = tuple(pltpu.VMEM(out.shape, out.dtype) for out in outs)
    args = (
        owner, resp_len, dt_bias, a_log, skip_d, x_raw, bc_raw, dt_raw, cotangent, ssm,
        conv_x_state.transpose(1, 0, 2), bc_state.transpose(1, 0, 2), conv_x_weight, bc_weight,
    )
    held = pl.pallas_call(
        functools.partial(kernel, peers, slices, groups),
        out_shape=staged,
        in_specs=[pl.BlockSpec(memory_space=pltpu.HBM)] * 14,
        out_specs=[vmem] * 6,
        scratch_shapes=[pltpu.SMEM(a.shape, a.dtype) for a in args[:5]]
        + [pltpu.VMEM(a.shape, a.dtype) for a in args[5:]]
        + [
            pltpu.VMEM((peers, depth + 1, channels + pair), BF16),
            pltpu.VMEM((peers, heads * width, nstate), BF16),
            pltpu.VMEM((slices, rows, pair), BF16),
            pltpu.VMEM((peers, depth + 1, channels + pair), BF16),
            pltpu.VMEM((peers, heads * width, nstate), BF16),
            pltpu.VMEM((responses, length + 8, channels), F32),
            pltpu.VMEM((responses, length + 8, pair), F32),
            pltpu.VMEM((responses, length + 8, channels), F32),
            pltpu.VMEM((responses, length + 8, pair), F32),
            pltpu.VMEM((responses, length, channels), F32),
            pltpu.VMEM((slices, rows, pair), F32),
            pltpu.VMEM((slices, rows, pair), F32),
            pltpu.VMEM((peers, rows_fin, max(channels, nstate)), F32),
            pltpu.VMEM((senders, 2 * depth + 2, nstate), F32),
            pltpu.VMEM((slices, 2 * depth + 2, nstate), F32),
            pltpu.VMEM((groups, 2 * depth + 2, nstate), F32),
            pltpu.VMEM((responses, length, channels), F32),
            pltpu.VMEM((responses, length, channels), F32),
            pltpu.VMEM((responses, length, nstate), F32),
            pltpu.VMEM((responses, depth + 1, length, nstate), F32),
            pltpu.VMEM((responses, heads, length, length), F32),
            pltpu.VMEM((responses, heads, length, length), F32),
            pltpu.VMEM((responses, length, length), F32),
            pltpu.VMEM((responses, 2, length, channels), BF16),
            dma((14,)),
        ]
        + [dma((2,))] * 7,
        compiler_params=pltpu.CompilerParams(
            collective_id=0, has_side_effects=True
        ),
    )(*args)
    anywhere = pl.BlockSpec(memory_space=pl.ANY)
    return pl.pallas_call(
        finish,
        out_shape=outs,
        in_specs=[vmem] * 6,
        out_specs=[anywhere] * 6,
        scratch_shapes=[dma((6,))],
        compiler_params=pltpu.CompilerParams(vmem_limit_bytes=16 * 1024 * 1024),
    )(*held)


def solution(mesh):
    in_specs = (
        P("exch", "dp"),
        P(("exch", "dp"), None),
        P("dp", "exch"),
        P("exch", "dp"),
        P("exch", "dp", None, None),
        P("exch", None, "dp"),
        P("exch", None, None),
        P("exch"),
        P("exch"),
        P(None, "dp"),
        P(),
        P("dp"),
        P("dp"),
        P("dp"),
    )
    out_specs = (
        P("exch", "dp"),
        P(("exch", "dp"), None),
        P("dp", "exch"),
        P(None, "dp"),
        P(),
        P(None, "dp"),
    )
    return jax.shard_map(local, mesh=mesh, in_specs=in_specs, out_specs=out_specs, check_vma=False)
```

```python
import functools

import jax
import jax.numpy as jnp
from jax import lax
from jax.experimental import pallas as pl
from jax.experimental.pallas import tpu as pltpu
from jax.sharding import PartitionSpec as P

DEV_GROUP = 8
AHEAD = 1
GROUP = 1
MESH = pl.DeviceIdType.MESH
F32 = jnp.float32
BF16 = jnp.bfloat16


def nn(a, b):
    return lax.dot_general(a, b, (((1,), (0,)), ((), ())), preferred_element_type=F32)


def nt(a, b):
    return lax.dot_general(a, b, (((1,), (1,)), ((), ())), preferred_element_type=F32)


def split(a):
    high = a.astype(BF16)
    return high, (a - high.astype(F32)).astype(BF16)


def two(dot, a, b):
    rows = a[0].shape[0]
    both = dot(jnp.concatenate(a, axis=0), b)
    return both[:rows] + both[rows:]


def three(dot, a, b):
    return two(dot, a, b[0]) + dot(a[0], b[1])


def iota(shape, dim):
    return lax.broadcasted_iota(jnp.int32, shape, dim)


def is_direct(peers, slices, groups):
    return groups == 1 and peers > 1 and peers * slices <= 64


def kernel(
    peers, slices, groups, *refs
):
    sources, refs = refs[:14], refs[14:]
    gx_ref, gbc_ref, gdt_ref, gwx_ref, gtaps_ref, gheads_ref = refs[:6]
    inputs, refs = refs[6:20], refs[20:]
    owner, lens, bias, a_log, skip, x_ref, bc_ref, dt_ref, cot_ref = inputs[:9]
    ssm_ref, cx_ref, cbc_ref, wx_ref, wbc_ref = inputs[9:]
    (
    msg, state, gath, msg_out, state_out, pad_x, pad_bc, dpx, dpbc, dw_ref, raw, back,
    fin, all_taps, across_taps, sum_taps, x_act, x_slope, bc_slope, tap_rows, decays, products, score_grads, fed,
    taken, sent,
    sem_in, sem_out, sem_msg, sem_state, sem_gath, sem_back, sem_fin, sem_along, sem_across,
    ) = refs
    mine = lax.axis_index("exch")
    me = lax.axis_index("dp")
    depth, prompts, channels = cx_ref.shape
    taps_n = depth + 1
    responses = lens.shape[0]
    heads = bias.shape[0]
    width = channels // heads
    tokens = x_ref.shape[0]
    length = tokens // responses
    rows = bc_ref.shape[0]
    pair = cbc_ref.shape[2]
    half = pair // 2
    lanes = responses * heads
    base = 8 - depth

    def along(offset):
        return {"exch": lax.rem(mine + offset, peers)}

    def spot(place):
        return {"dp": place % slices, "exch": place // slices}

    def add_up(terms):
        while len(terms) > 1:
            terms = [sum(terms[i + 1 : i + 2], terms[i]) for i in range(0, len(terms), 2)]
        return terms[0]

    devices = peers * slices
    direct = is_direct(peers, slices, groups)

    def across(offset):
        return {"dp": lax.rem(me + offset, slices)}

    barrier = pltpu.get_barrier_semaphore()
    for offset in range(1, peers):
        pl.semaphore_signal(barrier, inc=1, device_id=along(offset), device_id_type=MESH)
    for offset in range(1, slices):
        pl.semaphore_signal(barrier, inc=1, device_id=across(offset), device_id_type=MESH)
    sooner, later, blocks = (6, 0, 10, 11, 9), (1, 2, 3, 4), (5, 7, 8, 12, 13)
    loads = [
        pltpu.make_async_copy(src, dst, sem_in.at[0 if i in blocks else 1 + (sooner + later).index(i)])
        for i, (src, dst) in enumerate(zip(sources, inputs))
    ]
    for i in sooner:
        loads[i].start()
    for i in later + blocks:
        loads[i].start()
    for i in sooner[:-1]:
        loads[i].wait()
    tails = [
        jnp.concatenate([cx_ref[k].astype(F32), cbc_ref[k].astype(F32)], axis=1)
        for k in range(depth)
    ]

    def fill_msg(target, dst):
        small = [jnp.zeros((1, channels + pair), F32)] * depth
        flag = jnp.zeros((1, channels + pair), F32)
        for p in range(prompts):
            weight = (owner[p] == target).astype(F32)
            for k in range(depth):
                small[k] = small[k] + tails[k][p : p + 1] * weight
            flag = flag + weight
        dst[...] = jnp.concatenate(small + [flag], axis=0).astype(BF16)

    def fill_state(target, dst):
        big = jnp.zeros(ssm_ref.shape[1:], F32)
        for p in range(prompts):
            big = big + ssm_ref[p].astype(F32) * (owner[p] == target).astype(F32)
        dst[...] = big.astype(BF16)

    low = 1 - (2 * mine) // peers
    order = []
    for k in range(peers - 1):
        down = peers - 1 - k
        down = down - (mine - down + peers) // peers
        up = k + (k - mine + peers) // peers
        order.append(low * down + (1 - low) * up)

    for k in range(peers - 1):
        fill_msg(order[k], msg_out.at[k])
    fill_msg(mine, msg.at[mine])
    pl.semaphore_wait(barrier, slices - 1 + peers - 1)
    def remote(src, dst, sem, where):
        shared = sem.shape[0] == 1
        pltpu.make_async_remote_copy(
            src_ref=src,
            dst_ref=dst,
            send_sem=sem_out.at[0] if shared else sem.at[0],
            recv_sem=sem.at[0] if shared else sem.at[1],
            device_id=where,
            device_id_type=MESH,
        ).start()

    def settle(sem, which, ref):
        pltpu.make_async_copy(ref, ref, sem.at[which]).wait()

    def group_columns(ref, who):
        if groups == 1:
            return ref
        start = pl.multiple_of((who // DEV_GROUP) * pair, pair)
        return ref.at[:, pl.ds(start, pair)]

    for k in range(peers - 1):
        remote(msg_out.at[k], msg.at[mine], sem_msg, {"exch": order[k]})
    for o in range(1, slices):
        columns = group_columns(bc_ref, lax.rem(me + o, slices))
        remote(columns, gath.at[me], sem_gath, across(o))
    loads[sooner[-1]].wait()
    for k in range(peers - 1):
        fill_state(order[k], state_out.at[k])
        if k < AHEAD:
            remote(state_out.at[k], state.at[mine], sem_state, {"exch": order[k]})
    fill_state(mine, state.at[mine])

    def send_states():
        for k in range(AHEAD, peers - 1):
            remote(state_out.at[k], state.at[mine], sem_state, {"exch": order[k]})

    pl.when(lax.rem(me, 2) == 0)(send_states)
    gath[me] = group_columns(bc_ref, me)[...]
    for i in later:
        loads[i].wait()
    settle(sem_in, 0, taken)
    row_head = lax.rem(iota((lanes, 1), 0), heads)

    def per_row(ref):
        out = jnp.zeros((lanes, 1), F32)
        for h in range(heads):
            out = jnp.where(row_head == h, ref[h], out)
        return out

    lane_head = iota((1, channels), 1) // width
    skip_row = jnp.zeros((1, channels), F32)
    for h in range(heads):
        skip_row = jnp.where(lane_head == h, skip[h], skip_row)
    dt_in = jnp.concatenate(
        [dt_ref[:, r * length : (r + 1) * length].astype(F32) for r in range(responses)], axis=0
    )
    dt_pre = dt_in + per_row(bias)
    small = jnp.exp(-jnp.abs(dt_pre))
    above = 1.0 + small
    log1p = jnp.where(above == 1.0, small, jnp.log(above) * (small / (above - 1.0)))
    dt = jnp.maximum(dt_pre, 0.0) + log1p
    rate = jnp.exp(per_row(a_log))
    first = iota((length, length), 0)
    second = iota((length, length), 1)
    upto = (first <= second).astype(BF16)
    onward = (first >= second).astype(BF16)
    causal = first <= second

    def running(rows_in, ones):
        high = rows_in.astype(BF16).astype(F32)
        rest = rows_in - high
        middle = rest.astype(BF16).astype(F32)
        parts = nn(jnp.concatenate([high, middle, rest - middle], axis=0).astype(BF16), ones)
        return parts[:lanes] + (parts[lanes : 2 * lanes] + parts[2 * lanes :])

    logs = running(-rate * dt, upto)
    entry = jnp.exp(logs)
    logs_col = logs.T
    dt_col = dt.T
    entry_col = entry.T

    def spread_heads(cols, r):
        parts = [
            jnp.broadcast_to(cols[:, r * heads + h : r * heads + h + 1], (length, width))
            for h in range(heads)
        ]
        return jnp.concatenate(parts, axis=1)

    def indicator(r):
        row = iota((lanes, channels), 0)
        head = iota((lanes, channels), 1) // width
        return (row == r * heads + head).astype(BF16)

    wx = wx_ref[...]
    wbc = wbc_ref[...]

    def convolve(pad, weight, r, count):
        windows = [pad[r, base + k : base + k + count] for k in range(taps_n)]
        pre = windows[0] * weight[0:1]
        for k in range(1, taps_n):
            pre = pre + windows[k] * weight[k : k + 1]
        gate = 1.0 / (1.0 + jnp.exp(-pre))
        return pre * gate, gate * (1.0 + pre * (1.0 - gate)), windows

    cots, cots_b, dt_fulls = [], [], []
    for r in range(responses):
        block = slice(r * length, (r + 1) * length)
        pad_x[r, 0:8] = jnp.zeros((8, channels), F32)
        pad_x[r, 8 : 8 + length] = x_ref[block].astype(F32)
        live = iota((length, 1), 0) < lens[r]
        cots.append(jnp.where(live, cot_ref[block].astype(F32), 0.0))
        cots_b.append(cots[r].astype(BF16))
        dt_fulls.append(spread_heads(dt_col, r))
        x_act[r], x_slope[r], _ = convolve(pad_x, wx, r, length)
        weighted = split(x_act[r] * dt_fulls[r])
        total = jnp.zeros((length, length), F32)
        for h in range(heads):
            i = r * heads + h
            cols = slice(h * width, (h + 1) * width)
            gap = logs[i : i + 1] - logs_col[:, i : i + 1]
            decay = jnp.where(causal, jnp.exp(jnp.where(causal, gap, 0.0)), 0.0)
            cot_h = cots_b[r][:, cols]
            product = two(nt, [part[:, cols] for part in weighted], cot_h) * decay
            decays[r, h] = decay
            products[r, h] = product
            total = total + product
        score_grads[r] = total
        fed[r, 0:length], fed[r, length:] = split(cots[r] * spread_heads(entry_col, r))
    settle(sem_msg, 0, msg.at[pl.ds(0, peers - 1)])
    got = [msg[z].astype(F32) for z in range(peers)]
    weights = [[None] * peers for _ in range(prompts)]
    seen = jnp.zeros((1, channels + pair), F32)
    for z in range(peers):
        present = got[z][depth : depth + 1]
        for j in range(prompts):
            weights[j][z] = jnp.where(seen == float(j), present, 0.0)
        seen = seen + present
    for r in range(responses):
        prev = jnp.zeros((depth, channels + pair), F32)
        for z in range(peers):
            prev = prev + got[z][0:depth] * weights[r // GROUP][z]
        pad_x[r, base:8] = prev[:, :channels]
        pad_bc[r, base:8] = prev[:, channels:]

    grads, grads_t = [], []
    for r in range(responses):
        act, slope, _ = convolve(pad_x, wx, r, 8)
        x_act[r, 0:8] = act
        x_slope[r, 0:8] = slope
        scaled = act * dt_fulls[r][0:8]
        high = scaled.astype(BF16).astype(F32)
        stack = [
            jnp.where(lane_head == h, part, 0.0)
            for part in (high, scaled - high)
            for h in range(heads)
        ]
        both = nt(jnp.concatenate(stack, axis=0).astype(BF16), cots_b[r])
        total = jnp.zeros((8, length), F32)
        for h in range(heads):
            lower = 8 * (heads + h)
            product = (both[8 * h : 8 * h + 8] + both[lower : lower + 8]) * decays[r, h, 0:8]
            products[r, h, 0:8] = product
            total = total + product
        score_grads[r, 0:8] = total
        whole = score_grads[r]
        grads.append(split(whole))
        grads_t.append(split(whole.T))
    settle(sem_gath, 0, gath.at[pl.ds(0, slices - 1)])
    slots = length // rows
    for d in range(slices):
        r, place = d // slots, d % slots
        pad_bc[r, 8 + place * rows : 8 + (place + 1) * rows] = gath[d].astype(F32)

    def tap_sums(grad, windows):
        parts = [jnp.sum(grad * window, axis=0, keepdims=True) for window in windows]
        return jnp.concatenate(parts, axis=0)

    def input_grad(windows, weight, cols):
        total = windows[0] * weight[depth : depth + 1, cols]
        for j in range(1, taps_n):
            total = total + windows[j] * weight[depth - j : taps_n - j, cols]
        return total

    def send_bc(part):
        for r in range(responses):
            cols = slice(part * half, (part + 1) * half)
            block = input_grad([dpbc[r, j : j + length, cols] for j in range(taps_n)], wbc, cols)
            for place in range(slots):
                raw[part, r * slots + place] = block[place * rows : (place + 1) * rows]
        for o in range(1, slices):
            remote(raw.at[part, lax.rem(me + o, slices)], back.at[part, me], sem_back, across(o))
        back[part, me] = raw[part, me]

    projs = []
    b_taps = jnp.zeros((taps_n, half), F32)
    c_taps = jnp.zeros((taps_n, half), F32)
    for r in range(responses):
        act, slope, windows = convolve(pad_bc, wbc, r, length)
        proj_b, proj_c = split(act[:, :half]), split(act[:, half:])
        projs.append((proj_b, proj_c))
        pre_grad = three(nn, grads[r], proj_c) * slope[:, :half]
        c_grad = three(nn, grads_t[r], proj_b)
        dpbc[r, 0:length, 0:half] = pre_grad
        dpbc[r, 0:length, half:] = c_grad
        dpbc[r, length : length + 8] = jnp.zeros((8, pair), F32)
        bc_slope[r] = slope[:, half:]
        for k in range(taps_n):
            tap_rows[r, k] = slope[:, half:] * windows[k][:, half:]
        b_taps = b_taps + tap_sums(pre_grad, [window[:, :half] for window in windows])
        c_taps = c_taps + tap_sums(c_grad, [tap_rows[r, k] for k in range(taps_n)])

    place = mine * slices + me
    helper = slices + slices // 2 + 1
    is_helper = place == helper
    is_first = mine == 0
    slot = place if direct else mine

    def send_taps(part, value):
        all_taps[part, slot] = value
        block = all_taps.at[part, slot]
        if not direct:
            for o in range(1, peers):
                remote(block, block, sem_along, along(o))
            return
        for target in (0, 1, helper, *range(2, slices)):

            @pl.when(place != target)
            def _():
                remote(block, block, sem_along, spot(target))

    def sum_all():
        settle(sem_along, 1, all_taps.at[:, pl.ds(0, devices - 1)])
        for q in range(groups):
            sum_taps[q] = jnp.concatenate(
                [
                    add_up(
                        [
                            all_taps[part, z * slices + q * DEV_GROUP + d]
                            for z in range(peers)
                            for d in range(DEV_GROUP)
                        ]
                    )
                    for part in range(2)
                ],
                axis=0,
            )

    send_taps(0, b_taps)
    send_bc(0)

    pl.when(lax.rem(me, 2) == 1)(send_states)
    across_rows = jnp.zeros((lanes, length), F32)
    dt_first = jnp.zeros((lanes, length), F32)
    row_index = iota((lanes, 1), 0)
    skip_sum = jnp.zeros((1, channels), F32)
    grad_wx = jnp.zeros((taps_n, channels), F32)
    def local_rows(r, found_rows, dt_rows, skip_row_sum, taps_x):
        proj_b, proj_c = projs[r]
        scores = three(nt, proj_b, proj_c)
        for h in range(heads):
            i = r * heads + h
            cols = slice(h * width, (h + 1) * width)
            cot_h = cots_b[r][:, cols]
            dw_ref[r, :, cols] = two(nn, split(scores * decays[r, h]), cot_h)
            found = jnp.sum(scores * products[r, h], axis=0, keepdims=True)
            found_rows = jnp.where(row_index == i, found, found_rows)
        act, dw = x_act[r], dw_ref[r]
        prod = split(dw * act)
        mark = indicator(r)
        dt_rows = dt_rows + (nt(mark, prod[0]) + nt(mark, prod[1]))
        skip_row_sum = skip_row_sum + jnp.sum(cots[r] * act, axis=0, keepdims=True)
        pre_grad = (dw * dt_fulls[r] + skip_row * cots[r]) * x_slope[r]
        dpx[r, 0:length] = pre_grad
        dpx[r, length : length + 8] = jnp.zeros((8, channels), F32)
        windows = [pre_grad] + [dpx[r, j : j + length] for j in range(1, taps_n)]
        block = input_grad(windows, wx, slice(0, channels))
        gx_ref[r * length : (r + 1) * length] = block.astype(BF16)
        raw_x = pad_x[r, 8 : 8 + length]
        parts = []
        for j in range(depth, -1, -1):
            part = jnp.sum(windows[j] * raw_x, axis=0, keepdims=True)
            if j > 0:
                edge = dpx[r, 0:j] * pad_x[r, 8 - j : 8]
                part = part + jnp.sum(edge, axis=0, keepdims=True)
            parts.append(part)
        taps_x = taps_x + jnp.concatenate(parts, axis=0)
        return found_rows, dt_rows, skip_row_sum, taps_x

    sums = (across_rows, dt_first, skip_sum, grad_wx)
    for r in range(responses):
        sums = local_rows(r, *sums)
    settle(sem_state, 0, state.at[pl.ds(0, peers - 1)])
    starts, lates = [], []
    for r in range(responses):
        start = jnp.zeros(state.shape[1:], BF16)
        for z in range(peers):
            pick = weights[r // GROUP][z][:, : state.shape[2]].astype(BF16)
            start = start + state[z] * pick
        starts.append(start)
        both = nn(fed[r], start)
        late = both[:length] + both[length:]
        lates.append(late)
        c_taps = c_taps + tap_sums(late, [tap_rows[r, k] for k in range(taps_n)])
    send_taps(1, c_taps)
    across_rows, dt_first, skip_sum, grad_wx = sums
    entry_grad = jnp.zeros((lanes, length), F32)
    for r in range(responses):
        proj_c = projs[r][1]
        carried = two(nt, proj_c, starts[r])
        prod = split(carried * cots[r])
        mark = indicator(r)
        entry_grad = entry_grad + (nt(mark, prod[0]) + nt(mark, prod[1]))
    log_grad = across_rows + entry * entry_grad - dt * dt_first
    step_grad = running(log_grad, onward)
    dt_grad = dt_first - rate * step_grad
    raw_grad = dt_grad * (1.0 / (1.0 + jnp.exp(-dt_pre)))
    for r in range(responses):
        gdt_ref[:, r * length : (r + 1) * length] = raw_grad[
            r * heads : (r + 1) * heads
        ].astype(BF16)
    bias_rows = jnp.sum(raw_grad, axis=1, keepdims=True)
    decay_rows = -rate * jnp.sum(dt * step_grad, axis=1, keepdims=True)
    bias_grad = jnp.zeros((heads, 1), F32)
    decay_grad = jnp.zeros((heads, 1), F32)
    for r in range(responses):
        bias_grad = bias_grad + bias_rows[r * heads : (r + 1) * heads]
        decay_grad = decay_grad + decay_rows[r * heads : (r + 1) * heads]
    own = iota((heads, channels), 0) == iota((heads, channels), 1) // width
    skip_grad = jnp.sum(jnp.where(own, skip_sum, 0.0), axis=1, keepdims=True)
    at_head = iota((heads, half), 0) == iota((heads, half), 1)
    fin[mine] = jnp.zeros(fin.shape[1:], F32)
    fin[mine, 0:taps_n, 0:channels] = grad_wx
    for i, grad in enumerate((bias_grad, decay_grad, skip_grad)):
        row = jnp.sum(jnp.where(at_head, grad, 0.0), axis=0, keepdims=True)
        fin[mine, taps_n + i : taps_n + i + 1, 0:half] = row
    for o in range(1, peers):
        remote(fin.at[mine], fin.at[mine], sem_fin, along(o))

    for r in range(responses):
        dpbc[r, 0:length, half:] = (dpbc[r, 0:length, half:] + lates[r]) * bc_slope[r]
    send_bc(1)
    if direct:

        @pl.when(is_helper)
        def _():
            sum_all()
            for k in range(slices, devices):
                if k != helper:
                    remote(sum_taps, sum_taps, sem_across, spot(k))
    else:
        settle(sem_along, 1, all_taps.at[:, pl.ds(0, peers - 1)])
        across_taps[me] = jnp.concatenate(
            [add_up([all_taps[part, z] for z in range(peers)]) for part in range(2)], axis=0
        )
        for o in range(1, slices):
            remote(across_taps.at[me], across_taps.at[me], sem_across, across(o))
    settle(sem_back, 0, back.at[:, pl.ds(0, slices - 1)])
    for q in range(groups):
        for part in range(2):
            total = add_up([back[part, q * DEV_GROUP + d] for d in range(DEV_GROUP)])
            first_col = q * pair + part * half
            gbc_ref[:, first_col : first_col + half] = total.astype(BF16)
    settle(sem_fin, 0, fin.at[pl.ds(0, peers - 1)])
    total = fin[0]
    for z in range(1, peers):
        total = total + fin[z]
    gwx_ref[...] = total[0:taps_n, 0:channels]
    gheads_ref[...] = total[taps_n : taps_n + 3, 0:heads]

    settle(sem_out, 0, sent)
    if direct:

        @pl.when(is_helper)
        def _():
            settle(sem_along, 0, all_taps.at[:, pl.ds(0, slices)])
            settle(sem_across, 0, all_taps.at[:, pl.ds(0, devices - 1 - slices)])

        @pl.when(is_first)
        def _():
            settle(sem_along, 0, all_taps.at[:, pl.ds(0, slices)])
            sum_all()

        @pl.when(jnp.logical_not(jnp.logical_or(is_first, is_helper)))
        def _():
            settle(sem_along, 0, all_taps.at[:, pl.ds(0, slices + 1)])
            settle(sem_across, 1, sum_taps)
    else:
        settle(sem_along, 0, all_taps.at[:, pl.ds(0, peers - 1)])
        settle(sem_across, 0, across_taps.at[pl.ds(0, slices - 1)])
        settle(sem_across, 1, across_taps.at[pl.ds(0, slices - 1)])
        for q in range(groups):
            sum_taps[q] = add_up([across_taps[q * DEV_GROUP + d] for d in range(DEV_GROUP)])
    for q in range(groups):
        total = sum_taps[q]
        gtaps_ref[:, q * pair : q * pair + half] = total[0:taps_n]
        gtaps_ref[:, q * pair + half : (q + 1) * pair] = total[taps_n:]


def finish(*refs):
    count = len(refs) // 2
    sems = refs[-1]
    copies = [
        pltpu.make_async_copy(src, dst, sems.at[i])
        for i, (src, dst) in enumerate(zip(refs[:count], refs[count:-1]))
    ]
    for copy in copies:
        copy.start()
    for copy in copies:
        copy.wait()


def local(
    x_raw, bc_raw, dt_raw, cotangent, ssm_state, conv_x_state, conv_bc_state, owner, resp_len,
    conv_x_weight, conv_bc_weight, dt_bias, a_log, skip_d,
):
    peers = lax.axis_size("exch")
    slices = lax.axis_size("dp")
    prompts, heads, width, nstate = ssm_state.shape
    channels = x_raw.shape[1]
    pair = 2 * nstate
    depth = conv_x_state.shape[1]
    responses = resp_len.shape[0]
    tokens = x_raw.shape[0]
    length = tokens // responses
    rows, all_pairs = bc_raw.shape
    groups = all_pairs // pair
    bc_state, bc_weight = conv_bc_state, conv_bc_weight
    if groups > 1:
        first = (lax.axis_index("dp") // DEV_GROUP) * pair
        bc_state = lax.dynamic_slice_in_dim(conv_bc_state, first, pair, 2)
        bc_weight = lax.dynamic_slice_in_dim(conv_bc_weight, first, pair, 1)
    ssm = ssm_state.reshape(prompts, heads * width, nstate)
    senders = peers * slices if is_direct(peers, slices, groups) else peers
    rows_fin = -(-(depth + 4) // 8) * 8
    vmem = pl.BlockSpec(memory_space=pltpu.VMEM)
    dma = pltpu.SemaphoreType.DMA
    outs = (
        jax.ShapeDtypeStruct((tokens, channels), BF16),
        jax.ShapeDtypeStruct((rows, all_pairs), BF16),
        jax.ShapeDtypeStruct((heads, tokens), BF16),
        jax.ShapeDtypeStruct((depth + 1, channels), F32),
        jax.ShapeDtypeStruct((depth + 1, all_pairs), F32),
        jax.ShapeDtypeStruct((3, heads), F32),
    )
    staged = tuple(pltpu.VMEM(out.shape, out.dtype) for out in outs)
    args = (
        owner, resp_len, dt_bias, a_log, skip_d, x_raw, bc_raw, dt_raw, cotangent, ssm,
        conv_x_state.transpose(1, 0, 2), bc_state.transpose(1, 0, 2), conv_x_weight, bc_weight,
    )
    taken = sum(args[i].size * args[i].dtype.itemsize for i in (5, 7, 8, 12, 13))
    row = 4 * pair
    sent = (peers - 1) * (2 * (depth + 1) * (channels + pair) + 2 * heads * width * nstate)
    sent = sent + (peers - 1) * 4 * rows_fin * max(channels, nstate)
    sent = sent + (slices - 1) * (rows * row // 2 + rows * row)
    assert taken % 2048 == 0 and sent % 2048 == 0
    held = pl.pallas_call(
        functools.partial(kernel, peers, slices, groups),
        out_shape=staged,
        in_specs=[pl.BlockSpec(memory_space=pltpu.HBM)] * 14,
        out_specs=[vmem] * 6,
        scratch_shapes=[pltpu.SMEM(a.shape, a.dtype) for a in args[:5]]
        + [pltpu.VMEM(a.shape, a.dtype) for a in args[5:]]
        + [
            pltpu.VMEM((peers, depth + 1, channels + pair), BF16),
            pltpu.VMEM((peers, heads * width, nstate), BF16),
            pltpu.VMEM((slices, rows, pair), BF16),
            pltpu.VMEM((peers, depth + 1, channels + pair), BF16),
            pltpu.VMEM((peers, heads * width, nstate), BF16),
            pltpu.VMEM((responses, length + 8, channels), F32),
            pltpu.VMEM((responses, length + 8, pair), F32),
            pltpu.VMEM((responses, length + 8, channels), F32),
            pltpu.VMEM((responses, length + 8, pair), F32),
            pltpu.VMEM((responses, length, channels), F32),
            pltpu.VMEM((2, slices, rows, nstate), F32),
            pltpu.VMEM((2, slices, rows, nstate), F32),
            pltpu.VMEM((peers, rows_fin, max(channels, nstate)), F32),
            pltpu.VMEM((2, senders, depth + 1, nstate), F32),
            pltpu.VMEM((slices, 2 * depth + 2, nstate), F32),
            pltpu.VMEM((groups, 2 * depth + 2, nstate), F32),
            pltpu.VMEM((responses, length, channels), F32),
            pltpu.VMEM((responses, length, channels), F32),
            pltpu.VMEM((responses, length, nstate), F32),
            pltpu.VMEM((responses, depth + 1, length, nstate), F32),
            pltpu.VMEM((responses, heads, length, length), F32),
            pltpu.VMEM((responses, heads, length, length), F32),
            pltpu.VMEM((responses, length, length), F32),
            pltpu.VMEM((responses, 2 * length, channels), BF16),
            *(pltpu.VMEM((count // (4 * 128 * 4), 4, 128), F32) for count in (taken, sent)),
            dma((10,)),
        ]
        + [dma((1,))] * 6
        + [dma((2,))] * 2,
        compiler_params=pltpu.CompilerParams(
            collective_id=0, has_side_effects=True
        ),
    )(*args)
    anywhere = pl.BlockSpec(memory_space=pl.ANY)
    return pl.pallas_call(
        finish,
        out_shape=outs,
        in_specs=[vmem] * 6,
        out_specs=[anywhere] * 6,
        scratch_shapes=[dma((6,))],
        compiler_params=pltpu.CompilerParams(vmem_limit_bytes=16 * 1024 * 1024),
    )(*held)


def solution(mesh):
    in_specs = (
        P("exch", "dp"),
        P(("exch", "dp"), None),
        P("dp", "exch"),
        P("exch", "dp"),
        P("exch", "dp", None, None),
        P("exch", None, "dp"),
        P("exch", None, None),
        P("exch"),
        P("exch"),
        P(None, "dp"),
        P(),
        P("dp"),
        P("dp"),
        P("dp"),
    )
    out_specs = (
        P("exch", "dp"),
        P(("exch", "dp"), None),
        P("dp", "exch"),
        P(None, "dp"),
        P(),
        P(None, "dp"),
    )
    return jax.shard_map(local, mesh=mesh, in_specs=in_specs, out_specs=out_specs, check_vma=False)
```

```python
import functools

import jax
import jax.numpy as jnp
from jax import lax
from jax.experimental import pallas as pl
from jax.experimental.pallas import tpu as pltpu
from jax.sharding import PartitionSpec as P

DEV_GROUP = 8
GROUP = 1
MESH = pl.DeviceIdType.MESH
F32 = jnp.float32
BF16 = jnp.bfloat16


def nn(a, b):
    return lax.dot_general(a, b, (((1,), (0,)), ((), ())), preferred_element_type=F32)


def nt(a, b):
    return lax.dot_general(a, b, (((1,), (1,)), ((), ())), preferred_element_type=F32)


def split(a):
    high = a.astype(BF16)
    return high, (a - high.astype(F32)).astype(BF16)


def two(dot, a, b):
    rows = a[0].shape[0]
    both = dot(jnp.concatenate(a, axis=0), b)
    return both[:rows] + both[rows:]


def three(dot, a, b):
    return two(dot, a, b[0]) + dot(a[0], b[1])


def iota(shape, dim):
    return lax.broadcasted_iota(jnp.int32, shape, dim)


def is_direct(peers, slices, groups):
    return groups == 1 and peers > 1 and peers * slices <= 64


def kernel(
    peers, slices, groups, *refs
):
    sources, refs = refs[:14], refs[14:]
    gx_ref, gbc_ref, gdt_ref, gwx_ref, gtaps_ref, gheads_ref = refs[:6]
    inputs, refs = refs[6:20], refs[20:]
    owner, lens, bias, a_log, skip, x_ref, bc_ref, dt_ref, cot_ref = inputs[:9]
    ssm_ref, cx_ref, cbc_ref, wx_ref, wbc_ref = inputs[9:]
    (
    msg, state, gath, msg_out, state_out, pad_x, pad_bc, dpx, dpbc, dw_ref, raw, back,
    fin, all_taps, across_taps, sum_taps, x_act, x_slope, bc_slope, tap_rows, decays, products, score_grads, fed,
    taken, sent, starts, proj_rows, fence,
    sem_in, sem_out, sem_msg, sem_state, sem_gath, sem_back, sem_fin, sem_along, sem_across,
    ) = refs
    mine = lax.axis_index("exch")
    me = lax.axis_index("dp")
    depth, prompts, channels = cx_ref.shape
    taps_n = depth + 1
    responses = lens.shape[0]
    heads = bias.shape[0]
    width = channels // heads
    tokens = x_ref.shape[0]
    length = tokens // responses
    rows = bc_ref.shape[0]
    pair = cbc_ref.shape[2]
    half = pair // 2
    lanes = responses * heads
    base = 8 - depth

    def along(offset):
        return {"exch": lax.rem(mine + offset, peers)}

    def spot(place):
        return {"dp": place % slices, "exch": place // slices}

    def add_up(terms):
        while len(terms) > 1:
            terms = [sum(terms[i + 1 : i + 2], terms[i]) for i in range(0, len(terms), 2)]
        return terms[0]

    devices = peers * slices
    direct = is_direct(peers, slices, groups)

    def across(offset):
        return {"dp": lax.rem(me + offset, slices)}

    barrier = pltpu.get_barrier_semaphore()
    for offset in range(1, peers):
        pl.semaphore_signal(barrier, inc=1, device_id=along(offset), device_id_type=MESH)
    for offset in range(1, slices):
        pl.semaphore_signal(barrier, inc=1, device_id=across(offset), device_id_type=MESH)
    sooner, later, blocks = (6, 0, 10, 11, 9), (1, 2, 3, 4), (5, 7, 8, 12, 13)
    loads = [
        pltpu.make_async_copy(src, dst, sem_in.at[0 if i in blocks else 1 + (sooner + later).index(i)])
        for i, (src, dst) in enumerate(zip(sources, inputs))
    ]
    for i in sooner:
        loads[i].start()
    for i in later + blocks:
        loads[i].start()
    for i in sooner[:-1]:
        loads[i].wait()
    tails = [
        jnp.concatenate([cx_ref[k].astype(F32), cbc_ref[k].astype(F32)], axis=1)
        for k in range(depth)
    ]

    def fill_msg(target, dst):
        small = [jnp.zeros((1, channels + pair), F32)] * depth
        flag = jnp.zeros((1, channels + pair), F32)
        for p in range(prompts):
            weight = (owner[p] == target).astype(F32)
            for k in range(depth):
                small[k] = small[k] + tails[k][p : p + 1] * weight
            flag = flag + weight
        dst[...] = jnp.concatenate(small + [flag], axis=0).astype(BF16)

    def fill_state(target, dst):
        big = jnp.zeros(ssm_ref.shape[1:], F32)
        for p in range(prompts):
            big = big + ssm_ref[p].astype(F32) * (owner[p] == target).astype(F32)
        dst[...] = big.astype(BF16)

    low = 1 - (2 * mine) // peers
    order = []
    for k in range(peers - 1):
        down = peers - 1 - k
        down = down - (mine - down + peers) // peers
        up = k + (k - mine + peers) // peers
        order.append(low * down + (1 - low) * up)

    for k in range(peers - 1):
        fill_msg(order[k], msg_out.at[k])
    fill_msg(mine, msg.at[mine])
    pl.semaphore_wait(barrier, slices - 1 + peers - 1)
    def remote(src, dst, sem, where):
        shared = sem.shape[0] == 1
        pltpu.make_async_remote_copy(
            src_ref=src,
            dst_ref=dst,
            send_sem=sem_out.at[0] if shared else sem.at[0],
            recv_sem=sem.at[0] if shared else sem.at[1],
            device_id=where,
            device_id_type=MESH,
        ).start()

    def settle(sem, which, ref):
        pltpu.make_async_copy(ref, ref, sem.at[which]).wait()

    def group_columns(ref, who):
        if groups == 1:
            return ref
        start = pl.multiple_of((who // DEV_GROUP) * pair, pair)
        return ref.at[:, pl.ds(start, pair)]

    for k in range(peers - 1):
        remote(msg_out.at[k], msg.at[mine], sem_msg, {"exch": order[k]})
    for o in range(1, slices):
        columns = group_columns(bc_ref, lax.rem(me + o, slices))
        remote(columns, gath.at[me], sem_gath, across(o))
    loads[sooner[-1]].wait()
    for k in range(peers - 1):
        fill_state(order[k], state_out.at[k])
        remote(state_out.at[k], state.at[mine], sem_state, {"exch": order[k]})
    fill_state(mine, state.at[mine])
    gath[me] = group_columns(bc_ref, me)[...]
    for i in later:
        loads[i].wait()
    settle(sem_in, 0, taken)
    row_head = lax.rem(iota((lanes, 1), 0), heads)

    def per_row(ref):
        out = jnp.zeros((lanes, 1), F32)
        for h in range(heads):
            out = jnp.where(row_head == h, ref[h], out)
        return out

    lane_head = iota((1, channels), 1) // width
    skip_row = jnp.zeros((1, channels), F32)
    for h in range(heads):
        skip_row = jnp.where(lane_head == h, skip[h], skip_row)
    dt_in = jnp.concatenate(
        [dt_ref[:, r * length : (r + 1) * length].astype(F32) for r in range(responses)], axis=0
    )
    dt_pre = dt_in + per_row(bias)
    small = jnp.exp(-jnp.abs(dt_pre))
    above = 1.0 + small
    log1p = jnp.where(above == 1.0, small, jnp.log(above) * (small / (above - 1.0)))
    dt = jnp.maximum(dt_pre, 0.0) + log1p
    rate = jnp.exp(per_row(a_log))
    first = iota((length, length), 0)
    second = iota((length, length), 1)
    upto = (first <= second).astype(BF16)
    onward = (first >= second).astype(BF16)
    causal = first <= second

    def running(rows_in, ones):
        high = rows_in.astype(BF16).astype(F32)
        rest = rows_in - high
        middle = rest.astype(BF16).astype(F32)
        parts = nn(jnp.concatenate([high, middle, rest - middle], axis=0).astype(BF16), ones)
        return parts[:lanes] + (parts[lanes : 2 * lanes] + parts[2 * lanes :])

    logs = running(-rate * dt, upto)
    entry = jnp.exp(logs)
    logs_col = logs.T
    dt_col = dt.T
    entry_col = entry.T

    def spread_heads(cols, r):
        parts = [
            jnp.broadcast_to(cols[:, r * heads + h : r * heads + h + 1], (length, width))
            for h in range(heads)
        ]
        return jnp.concatenate(parts, axis=1)

    def indicator(r):
        row = iota((lanes, channels), 0)
        head = iota((lanes, channels), 1) // width
        return (row == r * heads + head).astype(BF16)

    wx = wx_ref[...]
    wbc = wbc_ref[...]

    def convolve(pad, weight, r, count):
        windows = [pad[r, base + k : base + k + count] for k in range(taps_n)]
        pre = windows[0] * weight[0:1]
        for k in range(1, taps_n):
            pre = pre + windows[k] * weight[k : k + 1]
        gate = 1.0 / (1.0 + jnp.exp(-pre))
        return pre * gate, gate * (1.0 + pre * (1.0 - gate)), windows

    cots, cots_b, dt_fulls = [], [], []
    for r in range(responses):
        block = slice(r * length, (r + 1) * length)
        pad_x[r, 0:8] = jnp.zeros((8, channels), F32)
        pad_x[r, 8 : 8 + length] = x_ref[block].astype(F32)
        live = iota((length, 1), 0) < lens[r]
        cots.append(jnp.where(live, cot_ref[block].astype(F32), 0.0))
        cots_b.append(cots[r].astype(BF16))
        dt_fulls.append(spread_heads(dt_col, r))
        x_act[r], x_slope[r], _ = convolve(pad_x, wx, r, length)
        weighted = split(x_act[r] * dt_fulls[r])
        total = jnp.zeros((length, length), F32)
        for h in range(heads):
            i = r * heads + h
            cols = slice(h * width, (h + 1) * width)
            gap = logs[i : i + 1] - logs_col[:, i : i + 1]
            decay = jnp.where(causal, jnp.exp(jnp.where(causal, gap, 0.0)), 0.0)
            cot_h = cots_b[r][:, cols]
            product = two(nt, [part[:, cols] for part in weighted], cot_h) * decay
            decays[r, h] = decay
            products[r, h] = product
            total = total + product
        score_grads[r] = total
        fed[r, 0:length], fed[r, length:] = split(cots[r] * spread_heads(entry_col, r))
    settle(sem_msg, 0, msg.at[pl.ds(0, peers - 1)])
    got = [msg[z].astype(F32) for z in range(peers)]
    weights = [[None] * peers for _ in range(prompts)]
    seen = jnp.zeros((1, channels + pair), F32)
    for z in range(peers):
        present = got[z][depth : depth + 1]
        for j in range(prompts):
            weights[j][z] = jnp.where(seen == float(j), present, 0.0)
        seen = seen + present
    for r in range(responses):
        prev = jnp.zeros((depth, channels + pair), F32)
        for z in range(peers):
            prev = prev + got[z][0:depth] * weights[r // GROUP][z]
        pad_x[r, base:8] = prev[:, :channels]
        pad_bc[r, base:8] = prev[:, channels:]

    grads, grads_t = [], []
    for r in range(responses):
        act, slope, _ = convolve(pad_x, wx, r, 8)
        x_act[r, 0:8] = act
        x_slope[r, 0:8] = slope
        scaled = act * dt_fulls[r][0:8]
        high = scaled.astype(BF16).astype(F32)
        stack = [
            jnp.where(lane_head == h, part, 0.0)
            for part in (high, scaled - high)
            for h in range(heads)
        ]
        both = nt(jnp.concatenate(stack, axis=0).astype(BF16), cots_b[r])
        total = jnp.zeros((8, length), F32)
        for h in range(heads):
            lower = 8 * (heads + h)
            product = (both[8 * h : 8 * h + 8] + both[lower : lower + 8]) * decays[r, h, 0:8]
            products[r, h, 0:8] = product
            total = total + product
        score_grads[r, 0:8] = total
        whole = score_grads[r]
        grads.append(split(whole))
        grads_t.append(split(whole.T))
    settle(sem_gath, 0, gath.at[pl.ds(0, slices - 1)])
    slots = length // rows
    for d in range(slices):
        r, place = d // slots, d % slots
        pad_bc[r, 8 + place * rows : 8 + (place + 1) * rows] = gath[d].astype(F32)

    def tap_sums(grad, windows):
        parts = [jnp.sum(grad * window, axis=0, keepdims=True) for window in windows]
        return jnp.concatenate(parts, axis=0)

    def input_grad(windows, weight, cols):
        total = windows[0] * weight[depth : depth + 1, cols]
        for j in range(1, taps_n):
            total = total + windows[j] * weight[depth - j : taps_n - j, cols]
        return total

    def send_bc(part):
        for r in range(responses):
            cols = slice(part * half, (part + 1) * half)
            block = input_grad([dpbc[r, j : j + length, cols] for j in range(taps_n)], wbc, cols)
            for place in range(slots):
                raw[part, r * slots + place] = block[place * rows : (place + 1) * rows]
        for o in range(1, slices):
            remote(raw.at[part, lax.rem(me + o, slices)], back.at[part, me], sem_back, across(o))
        back[part, me] = raw[part, me]

    projs = []
    b_taps = jnp.zeros((taps_n, half), F32)
    c_taps = jnp.zeros((taps_n, half), F32)
    for r in range(responses):
        act, slope, windows = convolve(pad_bc, wbc, r, length)
        proj_b, proj_c = split(act[:, :half]), split(act[:, half:])
        projs.append((proj_b, proj_c))
        proj_rows[r, 0:length], proj_rows[r, length:] = proj_c
        pre_grad = three(nn, grads[r], proj_c) * slope[:, :half]
        c_grad = three(nn, grads_t[r], proj_b)
        dpbc[r, 0:length, 0:half] = pre_grad
        dpbc[r, 0:length, half:] = c_grad
        dpbc[r, length : length + 8] = jnp.zeros((8, pair), F32)
        bc_slope[r] = slope[:, half:]
        for k in range(taps_n):
            tap_rows[r, k] = slope[:, half:] * windows[k][:, half:]
        b_taps = b_taps + tap_sums(pre_grad, [window[:, :half] for window in windows])
        c_taps = c_taps + tap_sums(c_grad, [tap_rows[r, k] for k in range(taps_n)])

    place = mine * slices + me
    helper = slices + slices // 2 + 1
    is_helper = place == helper
    is_first = mine == 0
    slot = place if direct else mine

    def send_taps(part, value):
        all_taps[part, slot] = value
        block = all_taps.at[part, slot]
        if not direct:
            for o in range(1, peers):
                remote(block, block, sem_along, along(o))
            return
        for target in (0, 1, helper, *range(2, slices)):

            @pl.when(place != target)
            def _():
                remote(block, block, sem_along, spot(target))

    def sum_all():
        settle(sem_along, 1, all_taps.at[:, pl.ds(0, devices - 1)])
        for q in range(groups):
            sum_taps[q] = jnp.concatenate(
                [
                    add_up(
                        [
                            all_taps[part, z * slices + q * DEV_GROUP + d]
                            for z in range(peers)
                            for d in range(DEV_GROUP)
                        ]
                    )
                    for part in range(2)
                ],
                axis=0,
            )

    send_taps(0, b_taps)
    send_bc(0)
    across_rows = jnp.zeros((lanes, length), F32)
    dt_first = jnp.zeros((lanes, length), F32)
    row_index = iota((lanes, 1), 0)
    skip_sum = jnp.zeros((1, channels), F32)
    grad_wx = jnp.zeros((taps_n, channels), F32)
    def local_rows(r, found_rows, dt_rows, skip_row_sum, taps_x):
        proj_b, proj_c = projs[r]
        scores = three(nt, proj_b, proj_c)
        for h in range(heads):
            i = r * heads + h
            cols = slice(h * width, (h + 1) * width)
            cot_h = cots_b[r][:, cols]
            dw_ref[r, :, cols] = two(nn, split(scores * decays[r, h]), cot_h)
            found = jnp.sum(scores * products[r, h], axis=0, keepdims=True)
            found_rows = jnp.where(row_index == i, found, found_rows)
        act, dw = x_act[r], dw_ref[r]
        prod = split(dw * act)
        mark = indicator(r)
        dt_rows = dt_rows + (nt(mark, prod[0]) + nt(mark, prod[1]))
        skip_row_sum = skip_row_sum + jnp.sum(cots[r] * act, axis=0, keepdims=True)
        pre_grad = (dw * dt_fulls[r] + skip_row * cots[r]) * x_slope[r]
        dpx[r, 0:length] = pre_grad
        dpx[r, length : length + 8] = jnp.zeros((8, channels), F32)
        windows = [pre_grad] + [dpx[r, j : j + length] for j in range(1, taps_n)]
        block = input_grad(windows, wx, slice(0, channels))
        gx_ref[r * length : (r + 1) * length] = block.astype(BF16)
        raw_x = pad_x[r, 8 : 8 + length]
        parts = []
        for j in range(depth, -1, -1):
            part = jnp.sum(windows[j] * raw_x, axis=0, keepdims=True)
            if j > 0:
                edge = dpx[r, 0:j] * pad_x[r, 8 - j : 8]
                part = part + jnp.sum(edge, axis=0, keepdims=True)
            parts.append(part)
        taps_x = taps_x + jnp.concatenate(parts, axis=0)
        return found_rows, dt_rows, skip_row_sum, taps_x

    sums = (across_rows, dt_first, skip_sum, grad_wx)
    for r in range(responses):
        sums = local_rows(r, *sums)
    settle(sem_state, 0, state.at[pl.ds(0, peers - 1)])
    lates = []
    for r in range(responses):
        start = jnp.zeros(state.shape[1:], BF16)
        for z in range(peers):
            pick = weights[r // GROUP][z][:, : state.shape[2]].astype(BF16)
            start = start + state[z] * pick
        starts[r] = start
        both = nn(fed[r], start)
        late = both[:length] + both[length:]
        lates.append(late)
        c_taps = c_taps + tap_sums(late, [tap_rows[r, k] for k in range(taps_n)])
    send_taps(1, c_taps)
    pl.semaphore_signal(fence, inc=1)
    pl.semaphore_wait(fence, 1)
    across_rows, dt_first, skip_sum, grad_wx = sums
    entry_grad = jnp.zeros((lanes, length), F32)
    for r in range(responses):
        both = nt(proj_rows[r], starts[r])
        carried = both[:length] + both[length:]
        prod = split(carried * cots[r])
        mark = indicator(r)
        entry_grad = entry_grad + (nt(mark, prod[0]) + nt(mark, prod[1]))
    log_grad = across_rows + entry * entry_grad - dt * dt_first
    step_grad = running(log_grad, onward)
    dt_grad = dt_first - rate * step_grad
    raw_grad = dt_grad * (1.0 / (1.0 + jnp.exp(-dt_pre)))
    for r in range(responses):
        gdt_ref[:, r * length : (r + 1) * length] = raw_grad[
            r * heads : (r + 1) * heads
        ].astype(BF16)
    bias_rows = jnp.sum(raw_grad, axis=1, keepdims=True)
    decay_rows = -rate * jnp.sum(dt * step_grad, axis=1, keepdims=True)
    bias_grad = jnp.zeros((heads, 1), F32)
    decay_grad = jnp.zeros((heads, 1), F32)
    for r in range(responses):
        bias_grad = bias_grad + bias_rows[r * heads : (r + 1) * heads]
        decay_grad = decay_grad + decay_rows[r * heads : (r + 1) * heads]
    own = iota((heads, channels), 0) == iota((heads, channels), 1) // width
    skip_grad = jnp.sum(jnp.where(own, skip_sum, 0.0), axis=1, keepdims=True)
    at_head = iota((heads, half), 0) == iota((heads, half), 1)
    fin[mine] = jnp.zeros(fin.shape[1:], F32)
    fin[mine, 0:taps_n, 0:channels] = grad_wx
    for i, grad in enumerate((bias_grad, decay_grad, skip_grad)):
        row = jnp.sum(jnp.where(at_head, grad, 0.0), axis=0, keepdims=True)
        fin[mine, taps_n + i : taps_n + i + 1, 0:half] = row
    for o in range(1, peers):
        remote(fin.at[mine], fin.at[mine], sem_fin, along(o))

    for r in range(responses):
        dpbc[r, 0:length, half:] = (dpbc[r, 0:length, half:] + lates[r]) * bc_slope[r]
    send_bc(1)
    if direct:

        @pl.when(is_helper)
        def _():
            sum_all()
            for k in range(slices, devices):
                if k != helper:
                    remote(sum_taps, sum_taps, sem_across, spot(k))
    else:
        settle(sem_along, 1, all_taps.at[:, pl.ds(0, peers - 1)])
        across_taps[me] = jnp.concatenate(
            [add_up([all_taps[part, z] for z in range(peers)]) for part in range(2)], axis=0
        )
        for o in range(1, slices):
            remote(across_taps.at[me], across_taps.at[me], sem_across, across(o))
    settle(sem_back, 0, back.at[:, pl.ds(0, slices - 1)])
    for q in range(groups):
        for part in range(2):
            total = add_up([back[part, q * DEV_GROUP + d] for d in range(DEV_GROUP)])
            first_col = q * pair + part * half
            gbc_ref[:, first_col : first_col + half] = total.astype(BF16)
    settle(sem_fin, 0, fin.at[pl.ds(0, peers - 1)])
    total = fin[0]
    for z in range(1, peers):
        total = total + fin[z]
    gwx_ref[...] = total[0:taps_n, 0:channels]
    gheads_ref[...] = total[taps_n : taps_n + 3, 0:heads]

    settle(sem_out, 0, sent)
    if direct:

        @pl.when(is_helper)
        def _():
            settle(sem_along, 0, all_taps.at[:, pl.ds(0, slices)])
            settle(sem_across, 0, all_taps.at[:, pl.ds(0, devices - 1 - slices)])

        @pl.when(is_first)
        def _():
            settle(sem_along, 0, all_taps.at[:, pl.ds(0, slices)])
            sum_all()

        @pl.when(jnp.logical_not(jnp.logical_or(is_first, is_helper)))
        def _():
            settle(sem_along, 0, all_taps.at[:, pl.ds(0, slices + 1)])
            settle(sem_across, 1, sum_taps)
    else:
        settle(sem_along, 0, all_taps.at[:, pl.ds(0, peers - 1)])
        settle(sem_across, 0, across_taps.at[pl.ds(0, slices - 1)])
        settle(sem_across, 1, across_taps.at[pl.ds(0, slices - 1)])
        for q in range(groups):
            sum_taps[q] = add_up([across_taps[q * DEV_GROUP + d] for d in range(DEV_GROUP)])
    for q in range(groups):
        total = sum_taps[q]
        gtaps_ref[:, q * pair : q * pair + half] = total[0:taps_n]
        gtaps_ref[:, q * pair + half : (q + 1) * pair] = total[taps_n:]


def finish(*refs):
    count = len(refs) // 2
    sems = refs[-1]
    copies = [
        pltpu.make_async_copy(src, dst, sems.at[i])
        for i, (src, dst) in enumerate(zip(refs[:count], refs[count:-1]))
    ]
    for copy in copies:
        copy.start()
    for copy in copies:
        copy.wait()


def local(
    x_raw, bc_raw, dt_raw, cotangent, ssm_state, conv_x_state, conv_bc_state, owner, resp_len,
    conv_x_weight, conv_bc_weight, dt_bias, a_log, skip_d,
):
    peers = lax.axis_size("exch")
    slices = lax.axis_size("dp")
    prompts, heads, width, nstate = ssm_state.shape
    channels = x_raw.shape[1]
    pair = 2 * nstate
    depth = conv_x_state.shape[1]
    responses = resp_len.shape[0]
    tokens = x_raw.shape[0]
    length = tokens // responses
    rows, all_pairs = bc_raw.shape
    groups = all_pairs // pair
    bc_state, bc_weight = conv_bc_state, conv_bc_weight
    if groups > 1:
        first = (lax.axis_index("dp") // DEV_GROUP) * pair
        bc_state = lax.dynamic_slice_in_dim(conv_bc_state, first, pair, 2)
        bc_weight = lax.dynamic_slice_in_dim(conv_bc_weight, first, pair, 1)
    ssm = ssm_state.reshape(prompts, heads * width, nstate)
    senders = peers * slices if is_direct(peers, slices, groups) else peers
    rows_fin = -(-(depth + 4) // 8) * 8
    vmem = pl.BlockSpec(memory_space=pltpu.VMEM)
    dma = pltpu.SemaphoreType.DMA
    outs = (
        jax.ShapeDtypeStruct((tokens, channels), BF16),
        jax.ShapeDtypeStruct((rows, all_pairs), BF16),
        jax.ShapeDtypeStruct((heads, tokens), BF16),
        jax.ShapeDtypeStruct((depth + 1, channels), F32),
        jax.ShapeDtypeStruct((depth + 1, all_pairs), F32),
        jax.ShapeDtypeStruct((3, heads), F32),
    )
    staged = tuple(pltpu.VMEM(out.shape, out.dtype) for out in outs)
    args = (
        owner, resp_len, dt_bias, a_log, skip_d, x_raw, bc_raw, dt_raw, cotangent, ssm,
        conv_x_state.transpose(1, 0, 2), bc_state.transpose(1, 0, 2), conv_x_weight, bc_weight,
    )
    taken = sum(args[i].size * args[i].dtype.itemsize for i in (5, 7, 8, 12, 13))
    row = 4 * pair
    sent = (peers - 1) * (2 * (depth + 1) * (channels + pair) + 2 * heads * width * nstate)
    sent = sent + (peers - 1) * 4 * rows_fin * max(channels, nstate)
    sent = sent + (slices - 1) * (rows * row // 2 + rows * row)
    assert taken % 2048 == 0 and sent % 2048 == 0
    held = pl.pallas_call(
        functools.partial(kernel, peers, slices, groups),
        out_shape=staged,
        in_specs=[pl.BlockSpec(memory_space=pltpu.HBM)] * 14,
        out_specs=[vmem] * 6,
        scratch_shapes=[pltpu.SMEM(a.shape, a.dtype) for a in args[:5]]
        + [pltpu.VMEM(a.shape, a.dtype) for a in args[5:]]
        + [
            pltpu.VMEM((peers, depth + 1, channels + pair), BF16),
            pltpu.VMEM((peers, heads * width, nstate), BF16),
            pltpu.VMEM((slices, rows, pair), BF16),
            pltpu.VMEM((peers, depth + 1, channels + pair), BF16),
            pltpu.VMEM((peers, heads * width, nstate), BF16),
            pltpu.VMEM((responses, length + 8, channels), F32),
            pltpu.VMEM((responses, length + 8, pair), F32),
            pltpu.VMEM((responses, length + 8, channels), F32),
            pltpu.VMEM((responses, length + 8, pair), F32),
            pltpu.VMEM((responses, length, channels), F32),
            pltpu.VMEM((2, slices, rows, nstate), F32),
            pltpu.VMEM((2, slices, rows, nstate), F32),
            pltpu.VMEM((peers, rows_fin, max(channels, nstate)), F32),
            pltpu.VMEM((2, senders, depth + 1, nstate), F32),
            pltpu.VMEM((slices, 2 * depth + 2, nstate), F32),
            pltpu.VMEM((groups, 2 * depth + 2, nstate), F32),
            pltpu.VMEM((responses, length, channels), F32),
            pltpu.VMEM((responses, length, channels), F32),
            pltpu.VMEM((responses, length, nstate), F32),
            pltpu.VMEM((responses, depth + 1, length, nstate), F32),
            pltpu.VMEM((responses, heads, length, length), F32),
            pltpu.VMEM((responses, heads, length, length), F32),
            pltpu.VMEM((responses, length, length), F32),
            pltpu.VMEM((responses, 2 * length, channels), BF16),
            *(pltpu.VMEM((count // (4 * 128 * 4), 4, 128), F32) for count in (taken, sent)),
            pltpu.VMEM((responses, heads * width, nstate), BF16),
            pltpu.VMEM((responses, 2 * length, nstate), BF16),
            pltpu.SemaphoreType.REGULAR,
            dma((10,)),
        ]
        + [dma((1,))] * 6
        + [dma((2,))] * 2,
        compiler_params=pltpu.CompilerParams(
            collective_id=0, has_side_effects=True
        ),
    )(*args)
    anywhere = pl.BlockSpec(memory_space=pl.ANY)
    return pl.pallas_call(
        finish,
        out_shape=outs,
        in_specs=[vmem] * 6,
        out_specs=[anywhere] * 6,
        scratch_shapes=[dma((6,))],
        compiler_params=pltpu.CompilerParams(vmem_limit_bytes=16 * 1024 * 1024),
    )(*held)


def solution(mesh):
    in_specs = (
        P("exch", "dp"),
        P(("exch", "dp"), None),
        P("dp", "exch"),
        P("exch", "dp"),
        P("exch", "dp", None, None),
        P("exch", None, "dp"),
        P("exch", None, None),
        P("exch"),
        P("exch"),
        P(None, "dp"),
        P(),
        P("dp"),
        P("dp"),
        P("dp"),
    )
    out_specs = (
        P("exch", "dp"),
        P(("exch", "dp"), None),
        P("dp", "exch"),
        P(None, "dp"),
        P(),
        P(None, "dp"),
    )
    return jax.shard_map(local, mesh=mesh, in_specs=in_specs, out_specs=out_specs, check_vma=False)
```

```python
import functools

import jax
import jax.numpy as jnp
from jax import lax
from jax.experimental import pallas as pl
from jax.experimental.pallas import tpu as pltpu
from jax.sharding import PartitionSpec as P

DEV_GROUP = 8
GROUP = 1
MESH = pl.DeviceIdType.MESH
F32 = jnp.float32
BF16 = jnp.bfloat16


def nn(a, b):
    return lax.dot_general(a, b, (((1,), (0,)), ((), ())), preferred_element_type=F32)


def nt(a, b):
    return lax.dot_general(a, b, (((1,), (1,)), ((), ())), preferred_element_type=F32)


def split(a):
    high = a.astype(BF16)
    return high, (a - high.astype(F32)).astype(BF16)


def two(dot, a, b):
    rows = a[0].shape[0]
    both = dot(jnp.concatenate(a, axis=0), b)
    return both[:rows] + both[rows:]


def three(dot, a, b):
    return two(dot, a, b[0]) + dot(a[0], b[1])


def iota(shape, dim):
    return lax.broadcasted_iota(jnp.int32, shape, dim)


def is_direct(peers, slices, groups):
    return groups == 1 and peers > 1 and peers * slices <= 64


def kernel(
    peers, slices, groups, *refs
):
    sources, refs = refs[:14], refs[14:]
    gx_ref, gbc_ref, gdt_ref, gwx_ref, gtaps_ref, gheads_ref = refs[:6]
    inputs, refs = refs[6:20], refs[20:]
    owner, lens, bias, a_log, skip, x_ref, bc_ref, dt_ref, cot_ref = inputs[:9]
    ssm_ref, cx_ref, cbc_ref, wx_ref, wbc_ref = inputs[9:]
    (
    msg, state, gath, msg_out, state_out, pad_x, pad_bc, dpx, dpbc, dw_ref, raw, back,
    fin, all_taps, across_taps, sum_taps, x_act, x_slope, bc_slope, tap_rows, decays, products, score_grads, fed,
    taken, sent, starts, proj_rows, fence,
    sem_in, sem_out, sem_msg, sem_state, sem_gath, sem_back, sem_fin, sem_along, sem_across,
    ) = refs
    mine = lax.axis_index("exch")
    me = lax.axis_index("dp")
    depth, prompts, channels = cx_ref.shape
    taps_n = depth + 1
    responses = lens.shape[0]
    heads = bias.shape[0]
    width = channels // heads
    tokens = x_ref.shape[0]
    length = tokens // responses
    rows = bc_ref.shape[0]
    pair = cbc_ref.shape[2]
    half = pair // 2
    lanes = responses * heads
    base = 8 - depth

    def along(offset):
        return {"exch": lax.rem(mine + offset, peers)}

    def spot(place):
        return {"dp": place % slices, "exch": place // slices}

    def add_up(terms):
        while len(terms) > 1:
            terms = [sum(terms[i + 1 : i + 2], terms[i]) for i in range(0, len(terms), 2)]
        return terms[0]

    devices = peers * slices
    direct = is_direct(peers, slices, groups)

    def across(offset):
        return {"dp": lax.rem(me + offset, slices)}

    barrier = pltpu.get_barrier_semaphore()
    for offset in range(1, peers):
        pl.semaphore_signal(barrier, inc=1, device_id=along(offset), device_id_type=MESH)
    for offset in range(1, slices):
        pl.semaphore_signal(barrier, inc=1, device_id=across(offset), device_id_type=MESH)
    sooner, later, blocks = (6, 0, 10, 11, 9), (1, 2, 3, 4), (5, 7, 8, 12, 13)
    loads = [
        pltpu.make_async_copy(src, dst, sem_in.at[0 if i in blocks else 1 + (sooner + later).index(i)])
        for i, (src, dst) in enumerate(zip(sources, inputs))
    ]
    for i in sooner:
        loads[i].start()
    for i in later + blocks:
        loads[i].start()
    for i in sooner[:-1]:
        loads[i].wait()
    tails = [
        jnp.concatenate([cx_ref[k].astype(F32), cbc_ref[k].astype(F32)], axis=1)
        for k in range(depth)
    ]

    def fill_msg(target, dst):
        small = [jnp.zeros((1, channels + pair), F32)] * depth
        flag = jnp.zeros((1, channels + pair), F32)
        for p in range(prompts):
            weight = (owner[p] == target).astype(F32)
            for k in range(depth):
                small[k] = small[k] + tails[k][p : p + 1] * weight
            flag = flag + weight
        dst[...] = jnp.concatenate(small + [flag], axis=0).astype(BF16)

    def fill_state(target, dst):
        big = jnp.zeros(ssm_ref.shape[1:], F32)
        for p in range(prompts):
            big = big + ssm_ref[p].astype(F32) * (owner[p] == target).astype(F32)
        dst[...] = big.astype(BF16)

    low = 1 - (2 * mine) // peers
    order = []
    for k in range(peers - 1):
        down = peers - 1 - k
        down = down - (mine - down + peers) // peers
        up = k + (k - mine + peers) // peers
        order.append(low * down + (1 - low) * up)

    for k in range(peers - 1):
        fill_msg(order[k], msg_out.at[k])
    fill_msg(mine, msg.at[mine])
    loads[sooner[-1]].wait()
    for k in range(peers - 1):
        fill_state(order[k], state_out.at[k])
    pl.semaphore_wait(barrier, slices - 1 + peers - 1)
    def remote(src, dst, sem, where):
        shared = sem.shape[0] == 1
        pltpu.make_async_remote_copy(
            src_ref=src,
            dst_ref=dst,
            send_sem=sem_out.at[0] if shared else sem.at[0],
            recv_sem=sem.at[0] if shared else sem.at[1],
            device_id=where,
            device_id_type=MESH,
        ).start()

    def settle(sem, which, ref):
        pltpu.make_async_copy(ref, ref, sem.at[which]).wait()

    def group_columns(ref, who):
        if groups == 1:
            return ref
        start = pl.multiple_of((who // DEV_GROUP) * pair, pair)
        return ref.at[:, pl.ds(start, pair)]

    for k in range(peers - 1):
        remote(msg_out.at[k], msg.at[mine], sem_msg, {"exch": order[k]})
    for k in range(peers - 1):
        remote(state_out.at[k], state.at[mine], sem_state, {"exch": order[k]})
    for o in range(1, slices):
        columns = group_columns(bc_ref, lax.rem(me + o, slices))
        remote(columns, gath.at[me], sem_gath, across(o))
    fill_state(mine, state.at[mine])
    gath[me] = group_columns(bc_ref, me)[...]
    for i in later:
        loads[i].wait()
    settle(sem_in, 0, taken)
    row_head = lax.rem(iota((lanes, 1), 0), heads)

    def per_row(ref):
        out = jnp.zeros((lanes, 1), F32)
        for h in range(heads):
            out = jnp.where(row_head == h, ref[h], out)
        return out

    lane_head = iota((1, channels), 1) // width
    skip_row = jnp.zeros((1, channels), F32)
    for h in range(heads):
        skip_row = jnp.where(lane_head == h, skip[h], skip_row)
    dt_in = jnp.concatenate(
        [dt_ref[:, r * length : (r + 1) * length].astype(F32) for r in range(responses)], axis=0
    )
    dt_pre = dt_in + per_row(bias)
    small = jnp.exp(-jnp.abs(dt_pre))
    above = 1.0 + small
    log1p = jnp.where(above == 1.0, small, jnp.log(above) * (small / (above - 1.0)))
    dt = jnp.maximum(dt_pre, 0.0) + log1p
    rate = jnp.exp(per_row(a_log))
    first = iota((length, length), 0)
    second = iota((length, length), 1)
    upto = (first <= second).astype(BF16)
    onward = (first >= second).astype(BF16)
    causal = first <= second

    def running(rows_in, ones):
        high = rows_in.astype(BF16).astype(F32)
        rest = rows_in - high
        middle = rest.astype(BF16).astype(F32)
        parts = nn(jnp.concatenate([high, middle, rest - middle], axis=0).astype(BF16), ones)
        return parts[:lanes] + (parts[lanes : 2 * lanes] + parts[2 * lanes :])

    logs = running(-rate * dt, upto)
    entry = jnp.exp(logs)
    logs_col = logs.T
    dt_col = dt.T
    entry_col = entry.T

    def spread_heads(cols, r):
        parts = [
            jnp.broadcast_to(cols[:, r * heads + h : r * heads + h + 1], (length, width))
            for h in range(heads)
        ]
        return jnp.concatenate(parts, axis=1)

    def indicator(r):
        row = iota((lanes, channels), 0)
        head = iota((lanes, channels), 1) // width
        return (row == r * heads + head).astype(BF16)

    wx = wx_ref[...]
    wbc = wbc_ref[...]

    def convolve(pad, weight, r, count):
        windows = [pad[r, base + k : base + k + count] for k in range(taps_n)]
        pre = windows[0] * weight[0:1]
        for k in range(1, taps_n):
            pre = pre + windows[k] * weight[k : k + 1]
        gate = 1.0 / (1.0 + jnp.exp(-pre))
        return pre * gate, gate * (1.0 + pre * (1.0 - gate)), windows

    cots, cots_b, dt_fulls = [], [], []
    for r in range(responses):
        block = slice(r * length, (r + 1) * length)
        pad_x[r, 0:8] = jnp.zeros((8, channels), F32)
        pad_x[r, 8 : 8 + length] = x_ref[block].astype(F32)
        live = iota((length, 1), 0) < lens[r]
        cots.append(jnp.where(live, cot_ref[block].astype(F32), 0.0))
        cots_b.append(cots[r].astype(BF16))
        dt_fulls.append(spread_heads(dt_col, r))
        x_act[r], x_slope[r], _ = convolve(pad_x, wx, r, length)
        weighted = split(x_act[r] * dt_fulls[r])
        total = jnp.zeros((length, length), F32)
        for h in range(heads):
            i = r * heads + h
            cols = slice(h * width, (h + 1) * width)
            gap = logs[i : i + 1] - logs_col[:, i : i + 1]
            decay = jnp.where(causal, jnp.exp(jnp.where(causal, gap, 0.0)), 0.0)
            cot_h = cots_b[r][:, cols]
            product = two(nt, [part[:, cols] for part in weighted], cot_h) * decay
            decays[r, h] = decay
            products[r, h] = product
            total = total + product
        score_grads[r] = total
        fed[r, 0:length], fed[r, length:] = split(cots[r] * spread_heads(entry_col, r))
    settle(sem_msg, 0, msg.at[pl.ds(0, peers - 1)])
    got = [msg[z].astype(F32) for z in range(peers)]
    weights = [[None] * peers for _ in range(prompts)]
    seen = jnp.zeros((1, channels + pair), F32)
    for z in range(peers):
        present = got[z][depth : depth + 1]
        for j in range(prompts):
            weights[j][z] = jnp.where(seen == float(j), present, 0.0)
        seen = seen + present
    for r in range(responses):
        prev = jnp.zeros((depth, channels + pair), F32)
        for z in range(peers):
            prev = prev + got[z][0:depth] * weights[r // GROUP][z]
        pad_x[r, base:8] = prev[:, :channels]
        pad_bc[r, base:8] = prev[:, channels:]

    grads, grads_t = [], []
    for r in range(responses):
        act, slope, _ = convolve(pad_x, wx, r, 8)
        x_act[r, 0:8] = act
        x_slope[r, 0:8] = slope
        scaled = act * dt_fulls[r][0:8]
        high = scaled.astype(BF16).astype(F32)
        stack = [
            jnp.where(lane_head == h, part, 0.0)
            for part in (high, scaled - high)
            for h in range(heads)
        ]
        both = nt(jnp.concatenate(stack, axis=0).astype(BF16), cots_b[r])
        total = jnp.zeros((8, length), F32)
        for h in range(heads):
            lower = 8 * (heads + h)
            product = (both[8 * h : 8 * h + 8] + both[lower : lower + 8]) * decays[r, h, 0:8]
            products[r, h, 0:8] = product
            total = total + product
        score_grads[r, 0:8] = total
        whole = score_grads[r]
        grads.append(split(whole))
        grads_t.append(split(whole.T))
    settle(sem_gath, 0, gath.at[pl.ds(0, slices - 1)])
    slots = length // rows
    for d in range(slices):
        r, place = d // slots, d % slots
        pad_bc[r, 8 + place * rows : 8 + (place + 1) * rows] = gath[d].astype(F32)

    def tap_sums(grad, windows):
        parts = [jnp.sum(grad * window, axis=0, keepdims=True) for window in windows]
        return jnp.concatenate(parts, axis=0)

    def input_grad(windows, weight, cols):
        total = windows[0] * weight[depth : depth + 1, cols]
        for j in range(1, taps_n):
            total = total + windows[j] * weight[depth - j : taps_n - j, cols]
        return total

    def send_bc(part):
        for r in range(responses):
            cols = slice(part * half, (part + 1) * half)
            block = input_grad([dpbc[r, j : j + length, cols] for j in range(taps_n)], wbc, cols)
            for place in range(slots):
                raw[part, r * slots + place] = block[place * rows : (place + 1) * rows]
        for o in range(1, slices):
            remote(raw.at[part, lax.rem(me + o, slices)], back.at[part, me], sem_back, across(o))
        back[part, me] = raw[part, me]

    projs = []
    b_taps = jnp.zeros((taps_n, half), F32)
    c_taps = jnp.zeros((taps_n, half), F32)
    for r in range(responses):
        act, slope, windows = convolve(pad_bc, wbc, r, length)
        proj_b, proj_c = split(act[:, :half]), split(act[:, half:])
        projs.append((proj_b, proj_c))
        proj_rows[r, 0:length], proj_rows[r, length:] = proj_c
        pre_grad = three(nn, grads[r], proj_c) * slope[:, :half]
        c_grad = three(nn, grads_t[r], proj_b)
        dpbc[r, 0:length, 0:half] = pre_grad
        dpbc[r, 0:length, half:] = c_grad
        dpbc[r, length : length + 8] = jnp.zeros((8, pair), F32)
        bc_slope[r] = slope[:, half:]
        for k in range(taps_n):
            tap_rows[r, k] = slope[:, half:] * windows[k][:, half:]
        b_taps = b_taps + tap_sums(pre_grad, [window[:, :half] for window in windows])
        c_taps = c_taps + tap_sums(c_grad, [tap_rows[r, k] for k in range(taps_n)])

    place = mine * slices + me
    helper = slices + slices // 2 + 1
    is_helper = place == helper
    is_first = mine == 0
    slot = place if direct else mine

    def send_taps(part, value):
        all_taps[part, slot] = value
        block = all_taps.at[part, slot]
        if not direct:
            for o in range(1, peers):
                remote(block, block, sem_along, along(o))
            return
        for target in (0, 1, helper, *range(2, slices)):

            @pl.when(place != target)
            def _():
                remote(block, block, sem_along, spot(target))

    def sum_all():
        settle(sem_along, 1, all_taps.at[:, pl.ds(0, devices - 1)])
        for q in range(groups):
            sum_taps[q] = jnp.concatenate(
                [
                    add_up(
                        [
                            all_taps[part, z * slices + q * DEV_GROUP + d]
                            for z in range(peers)
                            for d in range(DEV_GROUP)
                        ]
                    )
                    for part in range(2)
                ],
                axis=0,
            )

    send_taps(0, b_taps)
    send_bc(0)
    across_rows = jnp.zeros((lanes, length), F32)
    dt_first = jnp.zeros((lanes, length), F32)
    row_index = iota((lanes, 1), 0)
    skip_sum = jnp.zeros((1, channels), F32)
    grad_wx = jnp.zeros((taps_n, channels), F32)
    def local_rows(r, found_rows, dt_rows, skip_row_sum, taps_x):
        proj_b, proj_c = projs[r]
        scores = three(nt, proj_b, proj_c)
        for h in range(heads):
            i = r * heads + h
            cols = slice(h * width, (h + 1) * width)
            cot_h = cots_b[r][:, cols]
            dw_ref[r, :, cols] = two(nn, split(scores * decays[r, h]), cot_h)
            found = jnp.sum(scores * products[r, h], axis=0, keepdims=True)
            found_rows = jnp.where(row_index == i, found, found_rows)
        act, dw = x_act[r], dw_ref[r]
        prod = split(dw * act)
        mark = indicator(r)
        dt_rows = dt_rows + (nt(mark, prod[0]) + nt(mark, prod[1]))
        skip_row_sum = skip_row_sum + jnp.sum(cots[r] * act, axis=0, keepdims=True)
        pre_grad = (dw * dt_fulls[r] + skip_row * cots[r]) * x_slope[r]
        dpx[r, 0:length] = pre_grad
        dpx[r, length : length + 8] = jnp.zeros((8, channels), F32)
        windows = [pre_grad] + [dpx[r, j : j + length] for j in range(1, taps_n)]
        block = input_grad(windows, wx, slice(0, channels))
        gx_ref[r * length : (r + 1) * length] = block.astype(BF16)
        raw_x = pad_x[r, 8 : 8 + length]
        parts = []
        for j in range(depth, -1, -1):
            part = jnp.sum(windows[j] * raw_x, axis=0, keepdims=True)
            if j > 0:
                edge = dpx[r, 0:j] * pad_x[r, 8 - j : 8]
                part = part + jnp.sum(edge, axis=0, keepdims=True)
            parts.append(part)
        taps_x = taps_x + jnp.concatenate(parts, axis=0)
        return found_rows, dt_rows, skip_row_sum, taps_x

    sums = (across_rows, dt_first, skip_sum, grad_wx)
    for r in range(responses):
        sums = local_rows(r, *sums)
    settle(sem_state, 0, state.at[pl.ds(0, peers - 1)])
    lates = []
    for r in range(responses):
        start = jnp.zeros(state.shape[1:], BF16)
        for z in range(peers):
            pick = weights[r // GROUP][z][:, : state.shape[2]].astype(BF16)
            start = start + state[z] * pick
        starts[r] = start
        both = nn(fed[r], start)
        late = both[:length] + both[length:]
        lates.append(late)
        c_taps = c_taps + tap_sums(late, [tap_rows[r, k] for k in range(taps_n)])
    send_taps(1, c_taps)
    pl.semaphore_signal(fence, inc=1)
    pl.semaphore_wait(fence, 1)
    across_rows, dt_first, skip_sum, grad_wx = sums
    entry_grad = jnp.zeros((lanes, length), F32)
    for r in range(responses):
        both = nt(proj_rows[r], starts[r])
        carried = both[:length] + both[length:]
        prod = split(carried * cots[r])
        mark = indicator(r)
        entry_grad = entry_grad + (nt(mark, prod[0]) + nt(mark, prod[1]))
    log_grad = across_rows + entry * entry_grad - dt * dt_first
    step_grad = running(log_grad, onward)
    dt_grad = dt_first - rate * step_grad
    raw_grad = dt_grad * (1.0 / (1.0 + jnp.exp(-dt_pre)))
    for r in range(responses):
        gdt_ref[:, r * length : (r + 1) * length] = raw_grad[
            r * heads : (r + 1) * heads
        ].astype(BF16)
    bias_rows = jnp.sum(raw_grad, axis=1, keepdims=True)
    decay_rows = -rate * jnp.sum(dt * step_grad, axis=1, keepdims=True)
    bias_grad = jnp.zeros((heads, 1), F32)
    decay_grad = jnp.zeros((heads, 1), F32)
    for r in range(responses):
        bias_grad = bias_grad + bias_rows[r * heads : (r + 1) * heads]
        decay_grad = decay_grad + decay_rows[r * heads : (r + 1) * heads]
    own = iota((heads, channels), 0) == iota((heads, channels), 1) // width
    skip_grad = jnp.sum(jnp.where(own, skip_sum, 0.0), axis=1, keepdims=True)
    at_head = iota((heads, half), 0) == iota((heads, half), 1)
    fin[mine] = jnp.zeros(fin.shape[1:], F32)
    fin[mine, 0:taps_n, 0:channels] = grad_wx
    for i, grad in enumerate((bias_grad, decay_grad, skip_grad)):
        row = jnp.sum(jnp.where(at_head, grad, 0.0), axis=0, keepdims=True)
        fin[mine, taps_n + i : taps_n + i + 1, 0:half] = row
    for o in range(1, peers):
        remote(fin.at[mine], fin.at[mine], sem_fin, along(o))

    for r in range(responses):
        dpbc[r, 0:length, half:] = (dpbc[r, 0:length, half:] + lates[r]) * bc_slope[r]
    send_bc(1)
    if direct:

        @pl.when(is_helper)
        def _():
            sum_all()
            for k in range(slices, devices):
                if k != helper:
                    remote(sum_taps, sum_taps, sem_across, spot(k))
    else:
        settle(sem_along, 1, all_taps.at[:, pl.ds(0, peers - 1)])
        across_taps[me] = jnp.concatenate(
            [add_up([all_taps[part, z] for z in range(peers)]) for part in range(2)], axis=0
        )
        for o in range(1, slices):
            remote(across_taps.at[me], across_taps.at[me], sem_across, across(o))
    settle(sem_back, 0, back.at[:, pl.ds(0, slices - 1)])
    for q in range(groups):
        for part in range(2):
            total = add_up([back[part, q * DEV_GROUP + d] for d in range(DEV_GROUP)])
            first_col = q * pair + part * half
            gbc_ref[:, first_col : first_col + half] = total.astype(BF16)
    settle(sem_fin, 0, fin.at[pl.ds(0, peers - 1)])
    total = fin[0]
    for z in range(1, peers):
        total = total + fin[z]
    gwx_ref[...] = total[0:taps_n, 0:channels]
    gheads_ref[...] = total[taps_n : taps_n + 3, 0:heads]

    settle(sem_out, 0, sent)
    if direct:

        @pl.when(is_helper)
        def _():
            settle(sem_along, 0, all_taps.at[:, pl.ds(0, slices)])
            settle(sem_across, 0, all_taps.at[:, pl.ds(0, devices - 1 - slices)])

        @pl.when(is_first)
        def _():
            settle(sem_along, 0, all_taps.at[:, pl.ds(0, slices)])
            sum_all()

        @pl.when(jnp.logical_not(jnp.logical_or(is_first, is_helper)))
        def _():
            settle(sem_along, 0, all_taps.at[:, pl.ds(0, slices + 1)])
            settle(sem_across, 1, sum_taps)
    else:
        settle(sem_along, 0, all_taps.at[:, pl.ds(0, peers - 1)])
        settle(sem_across, 0, across_taps.at[pl.ds(0, slices - 1)])
        settle(sem_across, 1, across_taps.at[pl.ds(0, slices - 1)])
        for q in range(groups):
            sum_taps[q] = add_up([across_taps[q * DEV_GROUP + d] for d in range(DEV_GROUP)])
    for q in range(groups):
        total = sum_taps[q]
        gtaps_ref[:, q * pair : q * pair + half] = total[0:taps_n]
        gtaps_ref[:, q * pair + half : (q + 1) * pair] = total[taps_n:]


def finish(*refs):
    count = len(refs) // 2
    sems = refs[-1]
    copies = [
        pltpu.make_async_copy(src, dst, sems.at[i])
        for i, (src, dst) in enumerate(zip(refs[:count], refs[count:-1]))
    ]
    for copy in copies:
        copy.start()
    for copy in copies:
        copy.wait()


def local(
    x_raw, bc_raw, dt_raw, cotangent, ssm_state, conv_x_state, conv_bc_state, owner, resp_len,
    conv_x_weight, conv_bc_weight, dt_bias, a_log, skip_d,
):
    peers = lax.axis_size("exch")
    slices = lax.axis_size("dp")
    prompts, heads, width, nstate = ssm_state.shape
    channels = x_raw.shape[1]
    pair = 2 * nstate
    depth = conv_x_state.shape[1]
    responses = resp_len.shape[0]
    tokens = x_raw.shape[0]
    length = tokens // responses
    rows, all_pairs = bc_raw.shape
    groups = all_pairs // pair
    bc_state, bc_weight = conv_bc_state, conv_bc_weight
    if groups > 1:
        first = (lax.axis_index("dp") // DEV_GROUP) * pair
        bc_state = lax.dynamic_slice_in_dim(conv_bc_state, first, pair, 2)
        bc_weight = lax.dynamic_slice_in_dim(conv_bc_weight, first, pair, 1)
    ssm = ssm_state.reshape(prompts, heads * width, nstate)
    senders = peers * slices if is_direct(peers, slices, groups) else peers
    rows_fin = -(-(depth + 4) // 8) * 8
    vmem = pl.BlockSpec(memory_space=pltpu.VMEM)
    dma = pltpu.SemaphoreType.DMA
    outs = (
        jax.ShapeDtypeStruct((tokens, channels), BF16),
        jax.ShapeDtypeStruct((rows, all_pairs), BF16),
        jax.ShapeDtypeStruct((heads, tokens), BF16),
        jax.ShapeDtypeStruct((depth + 1, channels), F32),
        jax.ShapeDtypeStruct((depth + 1, all_pairs), F32),
        jax.ShapeDtypeStruct((3, heads), F32),
    )
    staged = tuple(pltpu.VMEM(out.shape, out.dtype) for out in outs)
    args = (
        owner, resp_len, dt_bias, a_log, skip_d, x_raw, bc_raw, dt_raw, cotangent, ssm,
        conv_x_state.transpose(1, 0, 2), bc_state.transpose(1, 0, 2), conv_x_weight, bc_weight,
    )
    taken = sum(args[i].size * args[i].dtype.itemsize for i in (5, 7, 8, 12, 13))
    row = 4 * pair
    sent = (peers - 1) * (2 * (depth + 1) * (channels + pair) + 2 * heads * width * nstate)
    sent = sent + (peers - 1) * 4 * rows_fin * max(channels, nstate)
    sent = sent + (slices - 1) * (rows * row // 2 + rows * row)
    assert taken % 2048 == 0 and sent % 2048 == 0
    held = pl.pallas_call(
        functools.partial(kernel, peers, slices, groups),
        out_shape=staged,
        in_specs=[pl.BlockSpec(memory_space=pltpu.HBM)] * 14,
        out_specs=[vmem] * 6,
        scratch_shapes=[pltpu.SMEM(a.shape, a.dtype) for a in args[:5]]
        + [pltpu.VMEM(a.shape, a.dtype) for a in args[5:]]
        + [
            pltpu.VMEM((peers, depth + 1, channels + pair), BF16),
            pltpu.VMEM((peers, heads * width, nstate), BF16),
            pltpu.VMEM((slices, rows, pair), BF16),
            pltpu.VMEM((peers, depth + 1, channels + pair), BF16),
            pltpu.VMEM((peers, heads * width, nstate), BF16),
            pltpu.VMEM((responses, length + 8, channels), F32),
            pltpu.VMEM((responses, length + 8, pair), F32),
            pltpu.VMEM((responses, length + 8, channels), F32),
            pltpu.VMEM((responses, length + 8, pair), F32),
            pltpu.VMEM((responses, length, channels), F32),
            pltpu.VMEM((2, slices, rows, nstate), F32),
            pltpu.VMEM((2, slices, rows, nstate), F32),
            pltpu.VMEM((peers, rows_fin, max(channels, nstate)), F32),
            pltpu.VMEM((2, senders, depth + 1, nstate), F32),
            pltpu.VMEM((slices, 2 * depth + 2, nstate), F32),
            pltpu.VMEM((groups, 2 * depth + 2, nstate), F32),
            pltpu.VMEM((responses, length, channels), F32),
            pltpu.VMEM((responses, length, channels), F32),
            pltpu.VMEM((responses, length, nstate), F32),
            pltpu.VMEM((responses, depth + 1, length, nstate), F32),
            pltpu.VMEM((responses, heads, length, length), F32),
            pltpu.VMEM((responses, heads, length, length), F32),
            pltpu.VMEM((responses, length, length), F32),
            pltpu.VMEM((responses, 2 * length, channels), BF16),
            *(pltpu.VMEM((count // (4 * 128 * 4), 4, 128), F32) for count in (taken, sent)),
            pltpu.VMEM((responses, heads * width, nstate), BF16),
            pltpu.VMEM((responses, 2 * length, nstate), BF16),
            pltpu.SemaphoreType.REGULAR,
            dma((10,)),
        ]
        + [dma((1,))] * 6
        + [dma((2,))] * 2,
        compiler_params=pltpu.CompilerParams(
            collective_id=0, has_side_effects=True
        ),
    )(*args)
    anywhere = pl.BlockSpec(memory_space=pl.ANY)
    return pl.pallas_call(
        finish,
        out_shape=outs,
        in_specs=[vmem] * 6,
        out_specs=[anywhere] * 6,
        scratch_shapes=[dma((6,))],
        compiler_params=pltpu.CompilerParams(vmem_limit_bytes=16 * 1024 * 1024),
    )(*held)


def solution(mesh):
    in_specs = (
        P("exch", "dp"),
        P(("exch", "dp"), None),
        P("dp", "exch"),
        P("exch", "dp"),
        P("exch", "dp", None, None),
        P("exch", None, "dp"),
        P("exch", None, None),
        P("exch"),
        P("exch"),
        P(None, "dp"),
        P(),
        P("dp"),
        P("dp"),
        P("dp"),
    )
    out_specs = (
        P("exch", "dp"),
        P(("exch", "dp"), None),
        P("dp", "exch"),
        P(None, "dp"),
        P(),
        P(None, "dp"),
    )
    return jax.shard_map(local, mesh=mesh, in_specs=in_specs, out_specs=out_specs, check_vma=False)
```
